32 devices in a mesh: grp: 4 (over y, x), shard: 8 (over z, core).
Axes of the slice: x: 2, y: 2, z: 4, core: 2. Of those that a mesh axis runs over, the one named last changes fastest.
Arguments:
- embeddings: bfloat16 [2048, 1280], P('shard'), may hold values from -6 to 6
- w_in: bfloat16 [1280, 2048], P('shard', 'grp'), may hold values from -0.15625 to 0.15625
- bias: bfloat16 [2048], P('grp'), may hold values from -3 to 3
- w_out: bfloat16 [2048], P('grp'), may hold values from -0.125 to 0.125
- pair_left: int32 [16384], P('shard'), may hold values from 0 to 255
- pair_home: int32 [16384, 1], P('shard'), may hold values from 0 to 7; in each aligned block of 2048 rows (0 to 2047, 2048 to 4095, ...) at most 512 rows name the same one
- pair_remote: int32 [16384], P('shard'), may hold values from 0 to 255
- outcome: int32 [16384], P('shard'), may hold values from 0 to 1
Outputs:
- grad_weight: float32 [1280, 2048], P('shard', 'grp')
- head_grads: float32 [2048, 2], P(('grp', 'shard'))
The draws below stay inside these ranges and needn't reach their ends.
Inputs may be any that keep to these rules, and one draw needn't show every extreme that they name: `pair_home`: among the pairs of one owner at most 512 have their second variant on one given index of shard, and in every draw some owner has exactly 512 with one index.
All inputs are finite; a program needn't handle non-finite values.
Results may differ from the reference program's by a relative error of at most 0.0016.
Values may be sent and summed in bfloat16 or wider, within the bound.
No kernel may reach another device: no remote copies, remote signals or barrier semaphores. Data moves between devices by JAX's collectives and lax.ppermute only.
A program may use at most 64 MiB of HBM per device.

```python
import math
import jax
import jax.numpy as jnp
import numpy as np
from jax import lax

D = 1280
HID = 2048
ROWS_DEV = 256
PAIRS_DEV = 2048
CAP = 512
ROWS = 2048
PAIRS = 16384
N_SHARD = 8


def place_ends(entries, stream_key, low, largest):
    spot = [jax.random.randint(jax.random.fold_in(stream_key, axis), (), 0, length) for axis, length in enumerate(entries.shape)]
    main_axis = entries.shape.index(max(entries.shape))
    next_to = spot[:main_axis] + [(spot[main_axis] + 1) % entries.shape[main_axis]] + spot[main_axis + 1:]
    return entries.at[tuple(spot)].set(low).at[tuple(next_to)].set(largest)


def steps_of(own_key, dims, shards, smallest, high):
    loudness = 1.0
    for position, blocks in shards:
        steps = jax.random.uniform(jax.random.fold_in(jax.random.fold_in(own_key, 6), position), (blocks,), jnp.float32, smallest / len(shards), high / len(shards))
        loudness = loudness * jnp.repeat(jnp.exp(steps), dims[position] // blocks).reshape((-1,) + (1,) * (len(dims) - 1 - position))
    return loudness


def shared_out(stream_key, own, number, rows, amount, top, reach, slope):
    ranking = jax.random.permutation(stream_key, amount)
    heavy_load, ordinary = shares(amount, rows * top, reach, slope, True), shares(amount, rows * top, reach, slope, False)
    places = jnp.arange(amount)

    def named(tallies, offset_by):
        used = int((tallies > 0).sum())
        fixed = max(1, used // 4)
        shifted = fixed + (places - fixed + offset_by * (used - fixed)) % max(1, amount - fixed)
        return jnp.zeros((amount,), jnp.int32).at[ranking[jnp.where(places < fixed, places, shifted)]].set(jnp.asarray(tallies, jnp.int32))

    tallies = jnp.where(number % 4 == 0, named(heavy_load, number // 4), named(ordinary, number - number // 4 - 1))
    mixed = jax.random.permutation(jax.random.fold_in(own, 3), amount)
    donor, taker = mixed[0:amount // 2 * 2:2], mixed[1:amount // 2 * 2:2]
    margin = jnp.minimum(tallies[donor] - 1, reach - tallies[taker]) // 2
    margin = jnp.where((donor == ranking[0]) | (taker == ranking[0]) | (tallies[taker] == 0), 0, jnp.maximum(margin, 0))
    shifted = jax.random.randint(jax.random.fold_in(own, 4), (amount // 2,), 0, 1 << 20) % (margin + 1)
    tallies = tallies.at[donor].add(-shifted).at[taker].add(shifted)
    members = jnp.searchsorted(jnp.cumsum(tallies), jnp.arange(rows * top), side="right").astype(jnp.int32)
    table = members.reshape(top, rows).T
    table = table[jax.random.permutation(jax.random.fold_in(own, 1), rows)]
    offset_by = jax.random.randint(jax.random.fold_in(own, 2), (rows, 1), 0, top)
    return jnp.take_along_axis(table, (jnp.arange(top)[None, :] + offset_by) % top, axis=1)


def shares(number_of, total, most, lean, full):
    weights = [(1 << 20) // math.isqrt(standing ** lean) + 1 for standing in range(1, number_of + 1)]
    largest = most if full else min(most, max(-(-total // number_of), total * weights[0] // sum(weights)))
    least = 1 if total - largest >= number_of - 1 else 0
    given, spare = [largest] + [least] * (number_of - 1), total - largest - least * (number_of - 1)
    while spare > 0:
        candidates = [i for i in range(1, number_of) if given[i] < largest] or [i for i in range(1, number_of) if given[i] < most]
        mass, remaining = sum([weights[i] for i in candidates]), spare
        for i in candidates:
            extra = min(most - given[i], max(1, remaining * weights[i] // mass), spare)
            given[i] = given[i] + extra
            spare = spare - extra
    return np.array(given)


def centred(key, extent, scale, reach, shards=(), kind=jnp.bfloat16):
    values = jax.random.normal(key, extent, jnp.float32) * scale
    if len(shards) > 0:
        values = steps_of(key, extent, shards, -0.22, 0.18) * values
    return jnp.clip(values, min=-reach, max=reach).astype(kind)


def setup_inputs(seed: int = 0) -> dict:
    streams_of = jax.random.split(jax.random.key(seed), 9)
    embeddings = centred(streams_of[0], (ROWS, D), 1.0, 6.0, ((0, 8),))
    w_in = centred(streams_of[1], (D, HID), D ** -0.5, 0.15625, ((0, 8), (1, 4)))
    bias = centred(streams_of[2], (HID,), 0.5, 3.0, ((0, 4),))
    w_out = centred(streams_of[3], (HID,), HID ** -0.5, 0.125, ((0, 4),))
    pair_left = place_ends(jax.random.randint(streams_of[4], (PAIRS,), 0, ROWS_DEV), jax.random.fold_in(streams_of[4], 1), 0, ROWS_DEV - 1).astype(jnp.int32)
    pair_home_keys = jax.random.split(jax.random.fold_in(streams_of[5], 1), PAIRS // PAIRS_DEV)
    pair_home_turns = jax.random.permutation(jax.random.fold_in(streams_of[5], 3), PAIRS // PAIRS_DEV)
    pair_home = jax.vmap(lambda own, number: shared_out(jax.random.fold_in(streams_of[5], 2), own, number, PAIRS_DEV, N_SHARD, 1, CAP, 2))(pair_home_keys, pair_home_turns).reshape((PAIRS, 1))
    pair_remote = place_ends(jax.random.randint(streams_of[6], (PAIRS,), 0, ROWS_DEV), jax.random.fold_in(streams_of[6], 1), 0, ROWS_DEV - 1).astype(jnp.int32)
    outcome = place_ends(jax.random.randint(streams_of[7], (PAIRS,), 0, 2), jax.random.fold_in(streams_of[7], 1), 0, 1).astype(jnp.int32)
    return {"embeddings": embeddings, "w_in": w_in, "bias": bias, "w_out": w_out, "pair_left": pair_left, "pair_home": pair_home, "pair_remote": pair_remote, "outcome": outcome}


def activate(values):
    return jax.nn.gelu(values, approximate=True)

def reference(embeddings, w_in, bias, w_out, pair_left, pair_home, pair_remote, outcome):
    blocks = embeddings.reshape(N_SHARD, ROWS_DEV, D)
    bias_f = bias.astype(jnp.float32)

    def forward(carry, block):
        pre = jnp.dot(block, w_in, preferred_element_type=jnp.float32) + bias_f
        hidden = activate(pre).astype(jnp.bfloat16)
        return (carry, jnp.dot(hidden, w_out, preferred_element_type=jnp.float32))
    _, scores = lax.scan(forward, jnp.zeros((), jnp.float32), blocks)
    scores = scores.reshape(-1)
    owner = jnp.arange(PAIRS_DEV * N_SHARD, dtype=jnp.int32) // PAIRS_DEV
    left = (owner * ROWS_DEV + pair_left).astype(jnp.int32)
    right = (pair_home[:, 0] * ROWS_DEV + pair_remote).astype(jnp.int32)
    resid = jax.nn.sigmoid(scores[left] - scores[right]) - outcome.astype(jnp.float32)
    dscore = jnp.zeros((ROWS_DEV * N_SHARD,), jnp.float32).at[left].add(resid).at[right].add(-resid)
    dblocks = dscore.reshape(N_SHARD, ROWS_DEV)
    w_out_f = w_out.astype(jnp.float32)

    def backward(carry, inputs):
        block, dblock = inputs
        grad_w, grad_b, grad_o = carry
        pre = jnp.dot(block, w_in, preferred_element_type=jnp.float32) + bias_f
        hidden = activate(pre).astype(jnp.bfloat16)
        _, pull = jax.vjp(activate, pre)
        dpre32 = pull(dblock[:, None] * w_out_f[None, :])[0]
        dpre = dpre32.astype(jnp.bfloat16)
        grad_w = grad_w + jnp.dot(block.T, dpre, preferred_element_type=jnp.float32)
        grad_b = grad_b + lax.optimization_barrier(jnp.sum(dpre32, axis=0))
        grad_o = grad_o + jnp.dot(dblock, hidden, precision=lax.Precision.HIGHEST, preferred_element_type=jnp.float32)
        return ((grad_w, grad_b, grad_o), 0)
    start = (jnp.zeros((D, HID), jnp.float32), jnp.zeros((HID,), jnp.float32), jnp.zeros((HID,), jnp.float32))
    (grad_w, grad_b, grad_o), _ = lax.scan(backward, start, (blocks, dblocks))
    return (grad_w, jnp.stack([grad_b, grad_o], axis=1))
```

```python
import jax
import jax.numpy as jnp
from jax import lax
from jax.experimental import pallas as pl
from jax.experimental.pallas import tpu as pltpu
from jax.sharding import PartitionSpec as P


F32 = jnp.float32
BF16 = jnp.bfloat16
LANES = 128
UNIT = 2.0**-12
TAIL = 16
NT = (((1,), (1,)), ((), ()))


def activate(values):
    return jax.nn.gelu(values, approximate=True)


def vmem():
    return pl.BlockSpec(memory_space=pltpu.VMEM)


def call(body, inputs, outputs, scratch=(), flops=0, name=None):
    return pl.pallas_call(
        body,
        out_shape=outputs,
        in_specs=[vmem()] * len(inputs),
        out_specs=[vmem()] * len(outputs),
        scratch_shapes=scratch,
        name=name,
        cost_estimate=pl.CostEstimate(flops=flops, bytes_accessed=1 << 20, transcendentals=0),
        compiler_params=pltpu.CompilerParams(vmem_limit_bytes=48 << 20),
    )(*inputs)


def one_hot(row, count, base, value):
    ids = lax.broadcasted_iota(jnp.int32, (count, LANES), 0)
    return jnp.where(ids == row - base, value, 0.0).astype(BF16)


def pair_rows(ref, part, chunk, chunks):
    at = part * chunks + chunk
    return ref[at : at + 1, :].astype(jnp.int32)


def weight_of(outcome):
    return jnp.where(outcome == 1, UNIT, 1.0)


def transpose_kernel(own, partner, out):
    core = lax.axis_index("shard") % 2
    rows = own.shape[0]
    for j, ref in enumerate((own, partner)):
        at = pl.multiple_of((core ^ j) * rows, rows)
        out[:, pl.ds(at, rows)] = ref[...].T


def left_kernel(own, partner, out, hot):
    core = lax.axis_index("shard") % 2
    rows = out.shape[0] // 2
    chunks = own.shape[0] // 3
    homes = out.shape[1] // rows
    for j, ref in enumerate((own, partner)):
        at = pl.multiple_of((core ^ j) * rows, rows)
        for q in range(chunks):
            weight = weight_of(pair_rows(ref, 2, q, chunks))
            hot[:, q * LANES : (q + 1) * LANES] = one_hot(pair_rows(ref, 0, q, chunks), rows, 0, weight)

        def home(h, carry, ref=ref, at=at):
            right = jnp.concatenate(
                [one_hot(pair_rows(ref, 1, q, chunks), rows, h * rows, 1.0) for q in range(chunks)], axis=1
            )
            out[pl.ds(at, rows), pl.ds(pl.multiple_of(h * rows, rows), rows)] = lax.dot_general(
                hot[...], right, NT, preferred_element_type=F32
            )
            return carry

        lax.fori_loop(0, homes, home, 0)


def right_kernel(*refs):
    n = len(refs) - 3
    lists, (lefts, out, signed) = refs[:n], refs[n:]
    shard = lax.axis_index("shard")
    rows = out.shape[0] // 2
    chunks = lists[0].shape[0] // 3
    base = (shard // 2) * (2 * rows)
    total = jnp.zeros((2 * rows, LANES), F32)
    for m, ref in enumerate(lists):
        at = pl.multiple_of((shard ^ m) * rows, rows)
        right = jnp.concatenate(
            [
                one_hot(pair_rows(ref, 1, q, chunks), 2 * rows, base, weight_of(pair_rows(ref, 2, q, chunks)))
                for q in range(chunks)
            ],
            axis=1,
        )
        left = jnp.concatenate(
            [one_hot(pair_rows(ref, 0, q, chunks), rows, 0, 1.0) for q in range(chunks)], axis=1
        )
        there = lax.dot_general(right, left, NT, preferred_element_type=F32)
        here = lefts[:, pl.ds(at, rows)]
        there_0, here_0 = jnp.floor(there), jnp.floor(here)
        there_1, here_1 = (there - there_0) * (0.5 / UNIT), (here - here_0) * (0.5 / UNIT)
        there_0, here_0 = there_0 * 0.5, here_0 * 0.5
        out[:, pl.ds(at, rows)] = (there_0 + there_1) + (here_0 + here_1)
        sign = (here_0 - here_1) - (there_0 - there_1)
        for q in range(rows // LANES):
            total = total + sign[:, q * LANES : (q + 1) * LANES]
    signed[...] = total


def forward_kernel(*refs):
    own, partner, bias, w_out = refs[:4]
    score, hidden, slope, gathered = refs[-4:]
    blocks = refs[4:-4]
    shard = lax.axis_index("shard")
    core = shard % 2
    rows = own.shape[0]
    depth = blocks[0].shape[0]
    half = hidden.shape[1]
    lane = pl.multiple_of(core * half, half)
    for m, ref in enumerate(blocks):
        at = pl.multiple_of((shard ^ m) * depth, depth)
        gathered[pl.ds(at, depth), :] = ref[:, pl.ds(lane, half)]
    shift = bias[:, pl.ds(lane, half)].astype(F32)
    weights = w_out[:, pl.ds(lane, half)]
    for j, ref in enumerate((own, partner)):
        at = pl.multiple_of((core ^ j) * rows, rows)
        pre = jnp.dot(ref[...], gathered[...], preferred_element_type=F32) + shift
        square = pre * pre
        scale = 0.7978845608028654
        t = jnp.tanh(scale * (pre + 0.044715 * (square * pre)))
        out = (pre * (0.5 * (1.0 + t))).astype(BF16)
        hidden[pl.ds(at, rows), :] = out
        slope[pl.ds(at, rows), :] = 0.5 * (1.0 + t) + (0.5 * pre) * (1.0 - t * t) * (
            scale * (1.0 + (3.0 * 0.044715) * square)
        )
        part = lax.dot_general(
            jnp.broadcast_to(weights, (8, half)), out, NT, preferred_element_type=F32
        )
        tiles = rows // LANES
        for q in range(tiles):
            piece = jnp.broadcast_to(part[0:1, q * LANES : (q + 1) * LANES], (score.shape[0], LANES))
            score[:, pl.ds((core ^ j) * tiles + q, 1), :] = piece.reshape(score.shape[0], 1, LANES)


def exponent_of(largest, limit):
    return jnp.maximum(jnp.ceil(jnp.log2(jnp.maximum(largest, 1e-30) * (1.0 / limit))), -100.0)


def coded(values):
    power = exponent_of(jnp.abs(values), 16000.0)
    scaled = values * jnp.exp2(-power)
    high = jnp.round(scaled)
    low = jnp.round((scaled - high) * 32000.0)
    return [power, high, low]


def decoded(rows, at):
    return (rows[at + 1 : at + 2, :] + rows[at + 2 : at + 3, :] * (1.0 / 32000.0)) * jnp.exp2(rows[at : at + 1, :])


def gradient_kernel(groups, *refs):
    received, counts, signed, flipped, hidden, slope, w_out = refs[:7]
    kept, heads = refs[7:9]
    messages = refs[9:-1]
    terms = refs[-1]
    shard = lax.axis_index("shard")
    chip, core = shard // 2, shard % 2
    n = len(messages) + 1
    rows = hidden.shape[0]
    half = hidden.shape[1]
    tiles = rows // LANES
    depth = kept.shape[0]
    lane = pl.multiple_of(core * half, half)

    def scores_of(z):
        parts = [received[g * n + 2 * z + k] for g in range(groups) for k in range(2)]
        while len(parts) > 1:
            parts = [a + b for a, b in zip(parts[::2], parts[1::2])]
        return parts[0] * 0.5

    across = [scores_of(z) for z in range(n // 2)]
    mine = scores_of(chip)
    turned = jnp.concatenate([mine, jnp.zeros((8 - tiles, LANES), F32)], axis=0).T
    weights = w_out[:, pl.ds(lane, half)].astype(F32)
    bias_sum = jnp.zeros((1, half), F32)
    score_sum = jnp.zeros((1, half), F32)
    sent = []
    for q in range(tiles):
        span = slice(q * LANES, (q + 1) * LANES)
        column = jnp.broadcast_to(turned[:, q : q + 1], (LANES, LANES))
        total = signed[span, :]
        for z in range(n // 2):
            for p in range(tiles):
                at = (z * tiles + p) * LANES
                total = total + counts[span, at : at + LANES] * jnp.tanh(column - across[z][p : p + 1, :])
        dscore = jnp.sum(total, axis=1, keepdims=True)
        dpre = (dscore * weights) * slope[span, :]
        bias_sum = bias_sum + jnp.sum(dpre, axis=0, keepdims=True)
        score_sum = score_sum + jnp.sum(dscore * hidden[span, :].astype(F32), axis=0, keepdims=True)
        sent.append(dpre.astype(BF16))
    terms[...] = jnp.dot(flipped[...], jnp.concatenate(sent, axis=0), preferred_element_type=F32)
    kept[...] = terms[pl.ds(pl.multiple_of(shard * depth, depth), depth), :]
    heads[...] = jnp.concatenate([bias_sum, score_sum], axis=0)
    extra = coded(bias_sum) + coded(score_sum)
    for m, ref in enumerate(messages, 1):
        block = terms[pl.ds(pl.multiple_of((shard ^ m) * depth, depth), depth), :]
        power = exponent_of(jnp.max(jnp.abs(block), axis=0, keepdims=True), 32000.0)
        ref[:depth, :] = jnp.round(block * jnp.exp2(-power)).astype(jnp.int32).astype(jnp.int16)
        pad = jnp.zeros((TAIL - 1 - len(extra), half), F32)
        tail = jnp.concatenate([power] + extra + [pad], axis=0)
        ref[depth:, :] = tail.astype(jnp.int32).astype(jnp.int16)


def sum_kernel(*refs):
    kept, heads = refs[:2]
    messages = refs[2:-2]
    weight, head = refs[-2:]
    shard = lax.axis_index("shard")
    core = shard % 2
    depth, half = kept.shape
    sums = [kept[...], jnp.zeros_like(kept)]
    tops = [heads[...], jnp.zeros_like(heads)]
    for m, ref in enumerate(messages, 1):
        tail = ref[depth:, :].astype(jnp.int32).astype(F32)
        sums[m % 2] = sums[m % 2] + ref[:depth, :].astype(jnp.int32).astype(F32) * jnp.exp2(tail[0:1, :])
        tops[m % 2] = tops[m % 2] + jnp.concatenate([decoded(tail, 1), decoded(tail, 4)], axis=0)
    weight[:, pl.ds(pl.multiple_of(core * half, half), half)] = sums[0]
    weight[:, pl.ds(pl.multiple_of((1 - core) * half, half), half)] = sums[1]
    units = head.shape[0]
    first = shard * units
    chosen = jnp.where(first // half == core, tops[0], tops[1])
    ids = lax.broadcasted_iota(jnp.int32, (units, half), 0) + first % half
    hit = ids == lax.broadcasted_iota(jnp.int32, (units, half), 1)
    for k in range(2):
        row = jnp.broadcast_to(chosen[k : k + 1, :], (units, half))
        head[:, k : k + 1] = jnp.sum(jnp.where(hit, row, 0.0), axis=1, keepdims=True)


def by_ppermute(embeddings, w_in, bias, w_out, pair_left, pair_home, pair_remote, outcome):
    rows, channels = embeddings.shape
    depth, hidden_units = w_in.shape
    half = hidden_units // 2
    n = lax.axis_size("shard")
    groups = lax.axis_size("grp")
    pair_count = pair_left.shape[0]
    chunks = pair_count // LANES

    def swap(value, m):
        return lax.ppermute(value, "shard", [(i, i ^ m) for i in range(n)])

    far = range(n - 2, 0, -2)

    def spread(value):
        got = {0: value}
        for m in far:
            got[m] = swap(value, m)
        for m in (0, *far):
            got[m + 1] = swap(got[m], 1)
        return [got[m] for m in range(n)]

    blocks = spread(w_in)
    right = pair_home[:, 0] * rows + pair_remote
    pairs = jnp.concatenate([pair_left, right, outcome]).astype(jnp.int16).reshape(3 * chunks, LANES)
    lists = spread(pairs)
    partner = swap(embeddings, 1)
    shape = jax.ShapeDtypeStruct
    (flipped,) = call(
        transpose_kernel, (embeddings, partner), [shape((channels, 2 * rows), BF16)], name="turn"
    )
    (lefts,) = call(
        left_kernel,
        (lists[0], lists[1]),
        [shape((2 * rows, n * rows), F32)],
        [pltpu.VMEM((rows, pair_count), BF16)],
        flops=4 * rows * n * rows * pair_count,
        name="left",
    )
    counts, signed = call(
        right_kernel,
        (*lists, lefts),
        [shape((2 * rows, n * rows), F32), shape((2 * rows, LANES), F32)],
        flops=4 * rows * n * rows * pair_count,
        name="right",
    )
    bias, w_out = bias.reshape(1, -1), w_out.reshape(1, -1)
    score, hidden, slope = call(
        forward_kernel,
        (embeddings, partner, bias, w_out, *blocks),
        [
            shape((groups * n, 2 * rows // LANES, LANES), F32),
            shape((2 * rows, half), BF16),
            shape((2 * rows, half), F32),
        ],
        [pltpu.VMEM((channels, half), BF16)],
        flops=4 * rows * channels * half,
        name="forward",
    )
    received = lax.all_to_all(score, ("grp", "shard"), 0, 0, tiled=True)
    message = shape((depth + TAIL, half), jnp.int16)
    kept, heads, *messages = call(
        lambda *refs: gradient_kernel(groups, *refs),
        (received, counts, signed, flipped, hidden, slope, w_out),
        [shape((depth, half), F32), shape((2, half), F32)] + [message] * (n - 1),
        [pltpu.VMEM((channels, half), F32)],
        flops=4 * rows * channels * half,
        name="gradient",
    )
    order = sorted(range(1, n), key=lambda m: -(m // 2))
    got = {m: swap(messages[m - 1], m) for m in order}
    weight, head = call(
        sum_kernel,
        (kept, heads, *[got[m] for m in range(1, n)]),
        [shape((depth, hidden_units), F32), shape((hidden_units // n, 2), F32)],
        name="total",
    )
    return weight, head


def by_collectives(embeddings, w_in, bias, w_out, pair_left, pair_home, pair_remote, outcome):
    local_rows = embeddings.shape[0]
    devices = lax.axis_size("shard")
    pair_count = pair_left.shape[0]
    capacity = 2 * pair_count // devices
    pre = jnp.dot(
        embeddings,
        lax.all_gather(w_in, "shard", axis=0, tiled=True),
        preferred_element_type=jnp.float32,
    )
    pre = pre + bias.astype(jnp.float32)[None, :]
    hidden = activate(pre).astype(jnp.bfloat16)
    part_score = jnp.dot(hidden, w_out, preferred_element_type=jnp.float32)
    score = lax.psum(part_score, "grp")
    home_dev = pair_home[:, 0]
    onehot = (home_dev[:, None] == jnp.arange(devices, dtype=jnp.int32)[None, :]).astype(jnp.int32)
    slot_index = jnp.sum(jnp.cumsum(onehot, axis=0) * onehot, axis=1) - 1
    request = jnp.zeros((devices, capacity), jnp.int32).at[home_dev, slot_index].set(pair_remote)
    wanted = lax.all_to_all(request, "shard", split_axis=0, concat_axis=0, tiled=True)
    wanted_rows = wanted.reshape(-1)
    outgoing = score[wanted_rows].reshape(devices, capacity)
    remote_score = lax.all_to_all(outgoing, "shard", split_axis=0, concat_axis=0, tiled=True)
    margin = score[pair_left] - remote_score[home_dev, slot_index]
    resid = jax.nn.sigmoid(margin) - outcome.astype(jnp.float32)
    backward_slots = (
        jnp.zeros((devices, capacity), jnp.float32).at[home_dev, slot_index].set(-resid)
    )
    returned = lax.all_to_all(backward_slots, "shard", split_axis=0, concat_axis=0, tiled=True)
    dscore = jax.ops.segment_sum(returned.reshape(-1), wanted_rows, num_segments=local_rows)
    dscore = dscore + jax.ops.segment_sum(resid, pair_left, num_segments=local_rows)
    _, pull = jax.vjp(activate, pre)
    dpre32 = pull(dscore[:, None] * w_out.astype(jnp.float32)[None, :])[0]
    dpre = dpre32.astype(jnp.bfloat16)
    grad_bias = jnp.sum(dpre32, axis=0)
    grad_score = jnp.dot(
        dscore, hidden, precision=lax.Precision.HIGHEST, preferred_element_type=jnp.float32
    )
    term_head = jnp.stack([grad_bias, grad_score], axis=1)
    term_weight = lax.dot_general(
        embeddings, dpre, (((0,), (0,)), ((), ())), preferred_element_type=jnp.float32
    )
    return (
        lax.psum_scatter(term_weight, "shard", scatter_dimension=0, tiled=True),
        lax.psum_scatter(term_head, "shard", scatter_dimension=0, tiled=True),
    )


def per_device(embeddings, w_in, bias, w_out, pair_left, pair_home, pair_remote, outcome):
    rows = embeddings.shape[0]
    depth, units = w_in.shape
    n = lax.axis_size("shard")
    small = (
        n & (n - 1) == 0
        and 2 <= n
        and n * rows <= 2048
        and rows % LANES == 0
        and 2 * rows <= 8 * LANES
        and depth % 16 == 0
        and units % (2 * LANES) == 0
        and pair_left.shape[0] % (16 * LANES) == 0
        and pair_left.shape[0] < 1 / UNIT
    )
    step = by_ppermute if small else by_collectives
    return step(embeddings, w_in, bias, w_out, pair_left, pair_home, pair_remote, outcome)


def solution(mesh):
    in_specs = (
        P("shard", None),
        P("shard", "grp"),
        P("grp"),
        P("grp"),
        P("shard"),
        P("shard", None),
        P("shard"),
        P("shard"),
    )
    out_specs = (P("shard", "grp"), P(("grp", "shard"), None))
    return jax.shard_map(
        per_device, mesh=mesh, in_specs=in_specs, out_specs=out_specs, check_vma=False
    )
```

```python
import functools

import jax
import jax.numpy as jnp
from jax import lax
from jax.experimental import pallas as pl
from jax.experimental.pallas import tpu as pltpu
from jax.sharding import PartitionSpec as P


F32 = jnp.float32
BF16 = jnp.bfloat16
LANES = 128
UNIT = 2.0**-12
TAIL = 8
NT = (((1,), (1,)), ((), ()))


def activate(values):
    return jax.nn.gelu(values, approximate=True)


def vmem():
    return pl.BlockSpec(memory_space=pltpu.VMEM)


def call(body, inputs, outputs, scratch=(), flops=0, space=pltpu.VMEM):
    return pl.pallas_call(
        body,
        out_shape=outputs,
        in_specs=[pl.BlockSpec(memory_space=space)] * len(inputs),
        out_specs=[vmem()] * len(outputs),
        scratch_shapes=scratch,
        cost_estimate=pl.CostEstimate(flops=flops, bytes_accessed=1 << 20, transcendentals=0),
        compiler_params=pltpu.CompilerParams(vmem_limit_bytes=24 << 20),
    )(*inputs)


def one_hot(row, count, value):
    ids = lax.broadcasted_iota(jnp.int32, (count, LANES), 0).astype(BF16)
    return jnp.where(ids == row.astype(BF16), value.astype(BF16), jnp.zeros((), BF16))


def pair_rows(ref, owner, part, chunk):
    return ref[owner, part, pl.ds(chunk, 1), :].astype(jnp.int32)


def weight_of(outcome):
    return jnp.where(outcome == 1, UNIT, 1.0)


def within(row, first, count):
    own = row - first
    return jnp.where((own >= 0) & (own < count), own, -1)


def transpose_kernel(own, partner, out):
    core = lax.axis_index("shard") % 2
    rows = own.shape[0]
    for j, ref in enumerate((own, partner)):
        at = pl.multiple_of((core ^ j) * rows, rows)
        out[:, pl.ds(at, rows)] = ref[...].T


def left_kernel(pairs, out, hot):
    rows = out.shape[0]
    chunks = pairs.shape[2]
    for q in range(chunks):
        weight = weight_of(pair_rows(pairs, 0, 2, q))
        hot[:, q * LANES : (q + 1) * LANES] = one_hot(pair_rows(pairs, 0, 0, q), rows, weight)
    ones = jnp.ones((1, LANES), F32)

    def home(h, carry):
        right = jnp.concatenate(
            [one_hot(within(pair_rows(pairs, 0, 1, q), h * rows, rows), rows, ones) for q in range(chunks)],
            axis=1,
        )
        out[:, pl.ds(pl.multiple_of(h * rows, rows), rows)] = lax.dot_general(
            hot[...], right, NT, preferred_element_type=F32
        )
        return carry

    lax.fori_loop(0, out.shape[1] // rows, home, 0)


def right_kernel(pairs, lefts, out):
    shard = lax.axis_index("shard")
    rows = out.shape[0]
    owners, _, chunks, _ = pairs.shape
    ones = jnp.ones((1, LANES), F32)
    total = jnp.zeros((rows, LANES), F32)
    for o in range(owners):
        at = slice(o * rows, (o + 1) * rows)
        right = jnp.concatenate(
            [
                one_hot(
                    within(pair_rows(pairs, o, 1, q), shard * rows, rows),
                    rows,
                    weight_of(pair_rows(pairs, o, 2, q)),
                )
                for q in range(chunks)
            ],
            axis=1,
        )
        left = jnp.concatenate([one_hot(pair_rows(pairs, o, 0, q), rows, ones) for q in range(chunks)], axis=1)
        there = lax.dot_general(right, left, NT, preferred_element_type=F32)
        here = lefts[:, at]
        there_0, here_0 = jnp.floor(there), jnp.floor(here)
        there_1, here_1 = (there - there_0) * (0.5 / UNIT), (here - here_0) * (0.5 / UNIT)
        there_0, here_0 = there_0 * 0.5, here_0 * 0.5
        out[:, at] = (there_0 + there_1) + (here_0 + here_1)
        sign = (here_0 - here_1) - (there_0 - there_1)
        for q in range(rows // LANES):
            total = total + sign[:, q * LANES : (q + 1) * LANES]
    out[:, owners * rows :] = total


def forward_kernel(*refs):
    own, partner, bias, w_out = refs[:4]
    score, hidden, slope, gathered = refs[-4:]
    blocks = refs[4:-4]
    shard = lax.axis_index("shard")
    core = shard % 2
    rows = own.shape[0]
    depth = blocks[0].shape[0]
    half = hidden.shape[1]
    lane = pl.multiple_of(core * half, half)
    for m, ref in enumerate(blocks):
        at = pl.multiple_of((shard ^ m) * depth, depth)
        gathered[pl.ds(at, depth), :] = ref[:, pl.ds(lane, half)]
    shift = bias[:, pl.ds(lane, half)].astype(F32)
    weights = w_out[:, pl.ds(lane, half)]
    for j, ref in enumerate((own, partner)):
        at = pl.multiple_of((core ^ j) * rows, rows)
        pre = jnp.dot(ref[...], gathered[...], preferred_element_type=F32) + shift
        square = pre * pre
        scale = 0.7978845608028654
        t = jnp.tanh(scale * (pre + 0.044715 * (square * pre)))
        out = (pre * (0.5 * (1.0 + t))).astype(BF16)
        hidden[pl.ds(at, rows), :] = out
        slope[pl.ds(at, rows), :] = 0.5 * (1.0 + t) + (0.5 * pre) * (1.0 - t * t) * (
            scale * (1.0 + (3.0 * 0.044715) * square)
        )
        part = lax.dot_general(
            jnp.broadcast_to(weights, (8, half)), out, NT, preferred_element_type=F32
        )
        tiles = rows // LANES
        for q in range(tiles):
            piece = jnp.broadcast_to(part[0:1, q * LANES : (q + 1) * LANES], (score.shape[0], LANES))
            score[:, pl.ds((core ^ j) * tiles + q, 1), :] = piece.reshape(score.shape[0], 1, LANES)


def exponent_of(largest, limit):
    return jnp.maximum(jnp.ceil(jnp.log2(jnp.maximum(largest, 1e-30) * (1.0 / limit))), -100.0)


def coded(values):
    power = exponent_of(jnp.abs(values), 16000.0)
    scaled = values * jnp.exp2(-power)
    high = jnp.round(scaled)
    low = jnp.round((scaled - high) * 32000.0)
    return [power, high, low]


def decoded(rows, at):
    return (rows[at + 1 : at + 2, :] + rows[at + 2 : at + 3, :] * (1.0 / 32000.0)) * jnp.exp2(rows[at : at + 1, :])


def pair_kernel(groups, received, counts, dscore):
    shard = lax.axis_index("shard")
    rows = counts.shape[0]
    n = (counts.shape[1] - LANES) // rows
    tiles = rows // LANES

    def scores_of(s):
        z, j = s // 2, s % 2
        parts = [
            received[g * n + 2 * z + k, pl.ds(j * tiles, tiles), :] for g in range(groups) for k in range(2)
        ]
        while len(parts) > 1:
            parts = [a + b for a, b in zip(parts[::2], parts[1::2])]
        return parts[0] * 0.5

    across = [scores_of(s) for s in range(n)]
    turned = jnp.concatenate([scores_of(shard), jnp.zeros((8 - tiles, LANES), F32)], axis=0).T
    for q in range(tiles):
        span = slice(q * LANES, (q + 1) * LANES)
        column = jnp.broadcast_to(turned[:, q : q + 1], (LANES, LANES))
        total = counts[span, n * rows :]
        for s in range(n):
            for p in range(tiles):
                at = (s * tiles + p) * LANES
                total = total + counts[span, at : at + LANES] * jnp.tanh(column - across[s][p : p + 1, :])
        dscore[span, :] = jnp.sum(total, axis=1, keepdims=True)


def gradient_kernel(*refs):
    near, next_to, flipped, hidden, slope, w_out = refs[:6]
    kept, heads = refs[6:8]
    messages = refs[8:-2]
    terms, sent = refs[-2:]
    shard = lax.axis_index("shard")
    core = shard % 2
    rows = near.shape[0]
    half = hidden.shape[1]
    depth = kept.shape[0]
    lane = pl.multiple_of(core * half, half)
    weights = w_out[:, pl.ds(lane, half)].astype(F32)
    bias_sum = jnp.zeros((1, half), F32)
    score_sum = jnp.zeros((1, half), F32)
    for j, ref in enumerate((near, next_to)):
        for r in range(rows // LANES):
            there = pl.ds(pl.multiple_of((core ^ j) * rows + r * LANES, LANES), LANES)
            dscore = ref[r * LANES : (r + 1) * LANES, :]
            dpre = (dscore * weights) * slope[there, :]
            bias_sum = bias_sum + jnp.sum(dpre, axis=0, keepdims=True)
            score_sum = score_sum + jnp.sum(dscore * hidden[there, :].astype(F32), axis=0, keepdims=True)
            sent[there, :] = dpre.astype(BF16)
    terms[...] = jnp.dot(flipped[...], sent[...], preferred_element_type=F32)
    kept[...] = terms[pl.ds(pl.multiple_of(shard * depth, depth), depth), :]
    heads[...] = jnp.concatenate([bias_sum, score_sum], axis=0)
    extra = coded(bias_sum) + coded(score_sum)
    for m, ref in enumerate(messages, 1):
        block = terms[pl.ds(pl.multiple_of((shard ^ m) * depth, depth), depth), :]
        power = exponent_of(jnp.max(jnp.abs(block), axis=0, keepdims=True), 32000.0)
        ref[:depth, :] = jnp.round(block * jnp.exp2(-power)).astype(jnp.int32).astype(jnp.int16)
        pad = jnp.zeros((TAIL - 1 - len(extra), half), F32)
        tail = jnp.concatenate([power] + extra + [pad], axis=0)
        ref[depth:, :] = tail.astype(jnp.int32).astype(jnp.int16)


def sum_kernel(*refs):
    kept, heads = refs[:2]
    messages = refs[2:-2]
    weight, head = refs[-2:]
    shard = lax.axis_index("shard")
    core = shard % 2
    depth, half = kept.shape
    sums = [kept[...], jnp.zeros_like(kept)]
    tops = [heads[...], jnp.zeros_like(heads)]
    for m, ref in enumerate(messages, 1):
        tail = ref[depth:, :].astype(jnp.int32).astype(F32)
        sums[m % 2] = sums[m % 2] + ref[:depth, :].astype(jnp.int32).astype(F32) * jnp.exp2(tail[0:1, :])
        tops[m % 2] = tops[m % 2] + jnp.concatenate([decoded(tail, 1), decoded(tail, 4)], axis=0)
    weight[:, pl.ds(pl.multiple_of(core * half, half), half)] = sums[0]
    weight[:, pl.ds(pl.multiple_of((1 - core) * half, half), half)] = sums[1]
    units = head.shape[1]
    first = shard * units
    chosen = jnp.where(first // half == core, tops[0], tops[1])
    chosen = jnp.concatenate([chosen, jnp.zeros((6, half), F32)], axis=0)
    head[...] = pltpu.roll(chosen, (half - first % half) % half, 1)[:2, :units]


def by_ppermute(embeddings, w_in, bias, w_out, pair_left, pair_home, pair_remote, outcome):
    rows, channels = embeddings.shape
    depth, hidden_units = w_in.shape
    half = hidden_units // 2
    n = lax.axis_size("shard")
    groups = lax.axis_size("grp")
    pair_count = pair_left.shape[0]
    chunks = pair_count // LANES

    def swap(value, m):
        return lax.ppermute(value, "shard", [(i, i ^ m) for i in range(n)])

    far = range(n - 2, 0, -2)

    def spread(value):
        got = {0: value}
        for m in far:
            got[m] = swap(value, m)
        for m in (0, *far):
            got[m + 1] = swap(got[m], 1)
        return [got[m] for m in range(n)]

    blocks = spread(w_in)
    tile = (1, 1, chunks, LANES)
    left, home, remote, result = (
        a.reshape(tile) for a in (pair_left, pair_home, pair_remote, outcome)
    )
    part = lax.broadcasted_iota(jnp.int32, (n, 3, chunks, LANES), 1)
    right = home * rows + remote
    pairs = jnp.where(part == 0, left, jnp.where(part == 1, right, result)).astype(jnp.int16)
    lists = lax.all_to_all(pairs, "shard", 0, 0, tiled=True)
    partner = swap(embeddings, 1)
    shape = jax.ShapeDtypeStruct
    (flipped,) = call(transpose_kernel, (embeddings, partner), [shape((channels, 2 * rows), BF16)])
    (lefts,) = call(
        left_kernel,
        (pairs,),
        [shape((rows, n * rows), F32)],
        [pltpu.VMEM((rows, pair_count), BF16)],
        flops=2 * rows * n * rows * pair_count,
    )
    (counts,) = call(
        right_kernel, (lists, lefts), [shape((rows, n * rows + LANES), F32)], flops=2 * rows * n * rows * pair_count
    )
    bias, w_out = bias.reshape(1, -1), w_out.reshape(1, -1)
    score, hidden, slope = call(
        forward_kernel,
        (embeddings, partner, bias, w_out, *blocks),
        [
            shape((groups * n, 2 * rows // LANES, LANES), F32),
            shape((2 * rows, half), BF16),
            shape((2 * rows, half), F32),
        ],
        [pltpu.VMEM((channels, half), BF16)],
        flops=4 * rows * channels * half,
    )
    received = lax.all_to_all(score, ("grp", "shard"), 0, 0, tiled=True)
    (near,) = call(
        functools.partial(pair_kernel, groups), (received, counts), [shape((rows, 1), F32)], flops=rows * n * rows
    )
    next_to = swap(near, 1)
    message = shape((depth + TAIL, half), jnp.int16)
    kept, heads, *messages = call(
        gradient_kernel,
        (near, next_to, flipped, hidden, slope, w_out),
        [shape((depth, half), F32), shape((2, half), F32)] + [message] * (n - 1),
        [pltpu.VMEM((channels, half), F32), pltpu.VMEM((2 * rows, half), BF16)],
        flops=4 * rows * channels * half,
    )
    order = sorted(range(1, n), key=lambda m: -(m // 2))
    got = {m: swap(messages[m - 1], m) for m in order}
    weight, head = call(
        sum_kernel,
        (kept, heads, *[got[m] for m in range(1, n)]),
        [shape((depth, hidden_units), F32), shape((2, hidden_units // n), F32)],
    )
    return weight, head.T


def by_collectives(embeddings, w_in, bias, w_out, pair_left, pair_home, pair_remote, outcome):
    local_rows = embeddings.shape[0]
    devices = lax.axis_size("shard")
    pair_count = pair_left.shape[0]
    capacity = 2 * pair_count // devices
    pre = jnp.dot(
        embeddings,
        lax.all_gather(w_in, "shard", axis=0, tiled=True),
        preferred_element_type=jnp.float32,
    )
    pre = pre + bias.astype(jnp.float32)[None, :]
    hidden = activate(pre).astype(jnp.bfloat16)
    part_score = jnp.dot(hidden, w_out, preferred_element_type=jnp.float32)
    score = lax.psum(part_score, "grp")
    home_dev = pair_home[:, 0]
    onehot = (home_dev[:, None] == jnp.arange(devices, dtype=jnp.int32)[None, :]).astype(jnp.int32)
    slot_index = jnp.sum(jnp.cumsum(onehot, axis=0) * onehot, axis=1) - 1
    request = jnp.zeros((devices, capacity), jnp.int32).at[home_dev, slot_index].set(pair_remote)
    wanted = lax.all_to_all(request, "shard", split_axis=0, concat_axis=0, tiled=True)
    wanted_rows = wanted.reshape(-1)
    outgoing = score[wanted_rows].reshape(devices, capacity)
    remote_score = lax.all_to_all(outgoing, "shard", split_axis=0, concat_axis=0, tiled=True)
    margin = score[pair_left] - remote_score[home_dev, slot_index]
    resid = jax.nn.sigmoid(margin) - outcome.astype(jnp.float32)
    backward_slots = (
        jnp.zeros((devices, capacity), jnp.float32).at[home_dev, slot_index].set(-resid)
    )
    returned = lax.all_to_all(backward_slots, "shard", split_axis=0, concat_axis=0, tiled=True)
    dscore = jax.ops.segment_sum(returned.reshape(-1), wanted_rows, num_segments=local_rows)
    dscore = dscore + jax.ops.segment_sum(resid, pair_left, num_segments=local_rows)
    _, pull = jax.vjp(activate, pre)
    dpre32 = pull(dscore[:, None] * w_out.astype(jnp.float32)[None, :])[0]
    dpre = dpre32.astype(jnp.bfloat16)
    grad_bias = jnp.sum(dpre32, axis=0)
    grad_score = jnp.dot(
        dscore, hidden, precision=lax.Precision.HIGHEST, preferred_element_type=jnp.float32
    )
    term_head = jnp.stack([grad_bias, grad_score], axis=1)
    term_weight = lax.dot_general(
        embeddings, dpre, (((0,), (0,)), ((), ())), preferred_element_type=jnp.float32
    )
    return (
        lax.psum_scatter(term_weight, "shard", scatter_dimension=0, tiled=True),
        lax.psum_scatter(term_head, "shard", scatter_dimension=0, tiled=True),
    )


def per_device(embeddings, w_in, bias, w_out, pair_left, pair_home, pair_remote, outcome):
    rows = embeddings.shape[0]
    depth, units = w_in.shape
    n = lax.axis_size("shard")
    small = (
        n & (n - 1) == 0
        and 2 <= n
        and n * rows <= 2048
        and rows % LANES == 0
        and 2 * rows <= 8 * LANES
        and depth % 16 == 0
        and units % (2 * LANES) == 0
        and pair_left.shape[0] % (16 * LANES) == 0
        and pair_left.shape[0] < 1 / UNIT
    )
    if not small:
        return by_collectives(
            embeddings, w_in, bias, w_out, pair_left, pair_home, pair_remote, outcome
        )
    return by_ppermute(
        embeddings, w_in, bias, w_out, pair_left, pair_home, pair_remote, outcome
    )


def solution(mesh):
    in_specs = (
        P("shard", None),
        P("shard", "grp"),
        P("grp"),
        P("grp"),
        P("shard"),
        P("shard", None),
        P("shard"),
        P("shard"),
    )
    out_specs = (P("shard", "grp"), P(("grp", "shard"), None))
    return jax.shard_map(
        per_device, mesh=mesh, in_specs=in_specs, out_specs=out_specs, check_vma=False
    )
```

```python
import functools

import jax
import jax.numpy as jnp
from jax import lax
from jax.experimental import pallas as pl
from jax.experimental.pallas import tpu as pltpu
from jax.sharding import PartitionSpec as P


F32 = jnp.float32
BF16 = jnp.bfloat16
LANES = 128
TAIL = 8
NT = (((1,), (1,)), ((), ()))


def activate(values):
    return jax.nn.gelu(values, approximate=True)


def vmem():
    return pl.BlockSpec(memory_space=pltpu.VMEM)


def call(body, inputs, outputs, scratch=(), flops=0, space=pltpu.VMEM):
    return pl.pallas_call(
        body,
        out_shape=outputs,
        in_specs=[pl.BlockSpec(memory_space=space)] * len(inputs),
        out_specs=[vmem()] * len(outputs),
        scratch_shapes=scratch,
        cost_estimate=pl.CostEstimate(flops=flops, bytes_accessed=1 << 20, transcendentals=0),
        compiler_params=pltpu.CompilerParams(vmem_limit_bytes=24 << 20),
    )(*inputs)


def pair_rows(ref, owner, part, chunk):
    return ref[owner, part, pl.ds(chunk, 1), :].astype(jnp.int32)


def transpose_kernel(own, partner, out):
    core = lax.axis_index("shard") % 2
    rows = own.shape[0]
    for j, ref in enumerate((own, partner)):
        at = pl.multiple_of((core ^ j) * rows, rows)
        out[:, pl.ds(at, rows)] = ref[...].T


def count_kernel(own, pairs, out, lefts):
    shard = lax.axis_index("shard")
    rows = out.shape[0]
    owners, _, chunks, _ = pairs.shape
    ids = lax.broadcasted_iota(jnp.int32, (rows, LANES), 0).astype(BF16)
    nought = jnp.zeros((), BF16)

    def table(ref, owner, home=None, sums=False):
        columns, added = [], jnp.zeros((rows, LANES), BF16)
        for q in range(chunks):
            row = pair_rows(ref, owner, 0, q)
            if home is not None:
                row = jnp.where(pair_rows(ref, owner, 1, q) == home, pair_rows(ref, owner, 2, q), -1)
            hit = ids == row.astype(BF16)
            columns.append(jnp.where(hit, jnp.ones((), BF16), nought).astype(jnp.float8_e5m2))
            if sums:
                half = jnp.where(pair_rows(ref, owner, 3, q) == 1, -0.5, 0.5).astype(BF16)
                added = added + jnp.where(hit, half, nought)
        return jnp.concatenate(columns, axis=1), added.astype(F32)

    lefts[...], total = table(own, 0, sums=True)
    for o in range(owners):
        here, _ = table(own, 0, home=o)
        there, added = table(pairs, o, home=shard, sums=True)
        theirs, _ = table(pairs, o)
        total = total - added
        out[:, o * rows : (o + 1) * rows] = 0.5 * (
            lax.dot_general(lefts[...], here, NT, preferred_element_type=F32)
            + lax.dot_general(there, theirs, NT, preferred_element_type=F32)
        )
    out[:, owners * rows :] = total


def forward_kernel(*refs):
    own, partner, bias, w_out = refs[:4]
    score, hidden, slope, gathered = refs[-4:]
    blocks = refs[4:-4]
    shard = lax.axis_index("shard")
    core = shard % 2
    rows = own.shape[0]
    depth = blocks[0].shape[0]
    half = hidden.shape[1]
    lane = pl.multiple_of(core * half, half)
    for m, ref in enumerate(blocks):
        at = pl.multiple_of((shard ^ m) * depth, depth)
        gathered[pl.ds(at, depth), :] = ref[:, pl.ds(lane, half)]
    shift = bias[:, pl.ds(lane, half)].astype(F32)
    weights = w_out[:, pl.ds(lane, half)]
    for j, ref in enumerate((own, partner)):
        at = pl.multiple_of((core ^ j) * rows, rows)
        pre = jnp.dot(ref[...], gathered[...], preferred_element_type=F32) + shift
        square = pre * pre
        scale = 0.7978845608028654
        t = jnp.tanh(scale * (pre + 0.044715 * (square * pre)))
        out = (pre * (0.5 * (1.0 + t))).astype(BF16)
        hidden[pl.ds(at, rows), :] = out
        slope[pl.ds(at, rows), :] = 0.5 * (1.0 + t) + (0.5 * pre) * (1.0 - t * t) * (
            scale * (1.0 + (3.0 * 0.044715) * square)
        )
        part = lax.dot_general(
            jnp.broadcast_to(weights, (8, half)), out, NT, preferred_element_type=F32
        )
        tiles = rows // LANES
        for q in range(tiles):
            piece = jnp.broadcast_to(part[0:1, q * LANES : (q + 1) * LANES], (score.shape[0], LANES))
            score[:, pl.ds((core ^ j) * tiles + q, 1), :] = piece.reshape(score.shape[0], 1, LANES)


def exponent_of(largest, limit):
    return jnp.maximum(jnp.ceil(jnp.log2(jnp.maximum(largest, 1e-30) * (1.0 / limit))), -100.0)


def coded(values):
    power = exponent_of(jnp.abs(values), 16000.0)
    scaled = values * jnp.exp2(-power)
    high = jnp.round(scaled)
    low = jnp.round((scaled - high) * 32000.0)
    return [power, high, low]


def decoded(rows, at):
    return (rows[at + 1 : at + 2, :] + rows[at + 2 : at + 3, :] * (1.0 / 32000.0)) * jnp.exp2(rows[at : at + 1, :])


def pair_kernel(groups, received, counts, dscore):
    shard = lax.axis_index("shard")
    rows = counts.shape[0]
    n = (counts.shape[1] - LANES) // rows
    tiles = rows // LANES

    def scores_of(s):
        z, j = s // 2, s % 2
        parts = [
            received[g * n + 2 * z + k, pl.ds(j * tiles, tiles), :] for g in range(groups) for k in range(2)
        ]
        while len(parts) > 1:
            parts = [a + b for a, b in zip(parts[::2], parts[1::2])]
        return parts[0] * 0.5

    across = [scores_of(s) for s in range(n)]
    turned = jnp.concatenate([scores_of(shard), jnp.zeros((8 - tiles, LANES), F32)], axis=0).T
    for q in range(tiles):
        span = slice(q * LANES, (q + 1) * LANES)
        column = jnp.broadcast_to(turned[:, q : q + 1], (LANES, LANES))
        total = counts[span, n * rows :]
        for s in range(n):
            for p in range(tiles):
                at = (s * tiles + p) * LANES
                total = total + counts[span, at : at + LANES] * jnp.tanh(column - across[s][p : p + 1, :])
        dscore[span, :] = jnp.sum(total, axis=1, keepdims=True)


def gradient_kernel(*refs):
    near, next_to, flipped, hidden, slope, w_out = refs[:6]
    kept, heads = refs[6:8]
    messages = refs[8:-2]
    terms, sent = refs[-2:]
    shard = lax.axis_index("shard")
    core = shard % 2
    rows = near.shape[0]
    half = hidden.shape[1]
    depth = kept.shape[0]
    lane = pl.multiple_of(core * half, half)
    weights = w_out[:, pl.ds(lane, half)].astype(F32)
    bias_sum = jnp.zeros((1, half), F32)
    score_sum = jnp.zeros((1, half), F32)
    for j, ref in enumerate((near, next_to)):
        for r in range(rows // LANES):
            there = pl.ds(pl.multiple_of((core ^ j) * rows + r * LANES, LANES), LANES)
            dscore = ref[r * LANES : (r + 1) * LANES, :]
            dpre = (dscore * weights) * slope[there, :]
            bias_sum = bias_sum + jnp.sum(dpre, axis=0, keepdims=True)
            score_sum = score_sum + jnp.sum(dscore * hidden[there, :].astype(F32), axis=0, keepdims=True)
            sent[there, :] = dpre.astype(BF16)
    terms[...] = jnp.dot(flipped[...], sent[...], preferred_element_type=F32)
    kept[...] = terms[pl.ds(pl.multiple_of(shard * depth, depth), depth), :]
    heads[...] = jnp.concatenate([bias_sum, score_sum], axis=0)
    extra = coded(bias_sum) + coded(score_sum)
    for m, ref in enumerate(messages, 1):
        block = terms[pl.ds(pl.multiple_of((shard ^ m) * depth, depth), depth), :]
        power = exponent_of(jnp.max(jnp.abs(block), axis=0, keepdims=True), 32000.0)
        ref[:depth, :] = jnp.round(block * jnp.exp2(-power)).astype(jnp.int32).astype(jnp.int16)
        pad = jnp.zeros((TAIL - 1 - len(extra), half), F32)
        tail = jnp.concatenate([power] + extra + [pad], axis=0)
        ref[depth:, :] = tail.astype(jnp.int32).astype(jnp.int16)


def sum_kernel(*refs):
    kept, heads = refs[:2]
    messages = refs[2:-2]
    weight, head = refs[-2:]
    shard = lax.axis_index("shard")
    core = shard % 2
    depth, half = kept.shape
    sums = [kept[...], jnp.zeros_like(kept)]
    tops = [heads[...], jnp.zeros_like(heads)]
    for m, ref in enumerate(messages, 1):
        tail = ref[depth:, :].astype(jnp.int32).astype(F32)
        sums[m % 2] = sums[m % 2] + ref[:depth, :].astype(jnp.int32).astype(F32) * jnp.exp2(tail[0:1, :])
        tops[m % 2] = tops[m % 2] + jnp.concatenate([decoded(tail, 1), decoded(tail, 4)], axis=0)
    weight[:, pl.ds(pl.multiple_of(core * half, half), half)] = sums[0]
    weight[:, pl.ds(pl.multiple_of((1 - core) * half, half), half)] = sums[1]
    units = head.shape[1]
    first = shard * units
    chosen = jnp.where(first // half == core, tops[0], tops[1])
    chosen = jnp.concatenate([chosen, jnp.zeros((6, half), F32)], axis=0)
    head[...] = pltpu.roll(chosen, (half - first % half) % half, 1)[:2, :units]


def by_ppermute(embeddings, w_in, bias, w_out, pair_left, pair_home, pair_remote, outcome):
    rows, channels = embeddings.shape
    depth, hidden_units = w_in.shape
    half = hidden_units // 2
    n = lax.axis_size("shard")
    groups = lax.axis_size("grp")
    pair_count = pair_left.shape[0]
    chunks = pair_count // LANES

    def swap(value, m):
        return lax.ppermute(value, "shard", [(i, i ^ m) for i in range(n)])

    far = range(n - 2, 0, -2)

    def spread(value):
        got = {0: value}
        for m in far:
            got[m] = swap(value, m)
        for m in (0, *far):
            got[m + 1] = swap(got[m], 1)
        return [got[m] for m in range(n)]

    blocks = spread(w_in)
    tile = (1, 1, chunks, LANES)
    columns = [a.reshape(tile) for a in (pair_left, pair_home, pair_remote, outcome)]
    part = lax.broadcasted_iota(jnp.int32, (n, 4, chunks, LANES), 1)
    pairs = columns[3]
    for k in (2, 1, 0):
        pairs = jnp.where(part == k, columns[k], pairs)
    pairs = pairs.astype(jnp.int16)
    lists = lax.all_to_all(pairs, "shard", 0, 0, tiled=True)
    partner = swap(embeddings, 1)
    shape = jax.ShapeDtypeStruct
    (flipped,) = call(transpose_kernel, (embeddings, partner), [shape((channels, 2 * rows), BF16)])
    (counts,) = call(
        count_kernel,
        (pairs, lists),
        [shape((rows, n * rows + LANES), F32)],
        [pltpu.VMEM((rows, pair_count), jnp.float8_e5m2)],
        flops=4 * rows * n * rows * pair_count,
    )
    bias, w_out = bias.reshape(1, -1), w_out.reshape(1, -1)
    score, hidden, slope = call(
        forward_kernel,
        (embeddings, partner, bias, w_out, *blocks),
        [
            shape((groups * n, 2 * rows // LANES, LANES), F32),
            shape((2 * rows, half), BF16),
            shape((2 * rows, half), F32),
        ],
        [pltpu.VMEM((channels, half), BF16)],
        flops=4 * rows * channels * half,
    )
    received = lax.all_to_all(score, ("grp", "shard"), 0, 0, tiled=True)
    (near,) = call(
        functools.partial(pair_kernel, groups), (received, counts), [shape((rows, 1), F32)], flops=rows * n * rows
    )
    next_to = swap(near, 1)
    message = shape((depth + TAIL, half), jnp.int16)
    kept, heads, *messages = call(
        gradient_kernel,
        (near, next_to, flipped, hidden, slope, w_out),
        [shape((depth, half), F32), shape((2, half), F32)] + [message] * (n - 1),
        [pltpu.VMEM((channels, half), F32), pltpu.VMEM((2 * rows, half), BF16)],
        flops=4 * rows * channels * half,
    )
    order = sorted(range(1, n), key=lambda m: -(m // 2))
    got = {m: swap(messages[m - 1], m) for m in order}
    weight, head = call(
        sum_kernel,
        (kept, heads, *[got[m] for m in range(1, n)]),
        [shape((depth, hidden_units), F32), shape((2, hidden_units // n), F32)],
    )
    return weight, head.T


def by_collectives(embeddings, w_in, bias, w_out, pair_left, pair_home, pair_remote, outcome):
    local_rows = embeddings.shape[0]
    devices = lax.axis_size("shard")
    pair_count = pair_left.shape[0]
    capacity = 2 * pair_count // devices
    pre = jnp.dot(
        embeddings,
        lax.all_gather(w_in, "shard", axis=0, tiled=True),
        preferred_element_type=jnp.float32,
    )
    pre = pre + bias.astype(jnp.float32)[None, :]
    hidden = activate(pre).astype(jnp.bfloat16)
    part_score = jnp.dot(hidden, w_out, preferred_element_type=jnp.float32)
    score = lax.psum(part_score, "grp")
    home_dev = pair_home[:, 0]
    onehot = (home_dev[:, None] == jnp.arange(devices, dtype=jnp.int32)[None, :]).astype(jnp.int32)
    slot_index = jnp.sum(jnp.cumsum(onehot, axis=0) * onehot, axis=1) - 1
    request = jnp.zeros((devices, capacity), jnp.int32).at[home_dev, slot_index].set(pair_remote)
    wanted = lax.all_to_all(request, "shard", split_axis=0, concat_axis=0, tiled=True)
    wanted_rows = wanted.reshape(-1)
    outgoing = score[wanted_rows].reshape(devices, capacity)
    remote_score = lax.all_to_all(outgoing, "shard", split_axis=0, concat_axis=0, tiled=True)
    margin = score[pair_left] - remote_score[home_dev, slot_index]
    resid = jax.nn.sigmoid(margin) - outcome.astype(jnp.float32)
    backward_slots = (
        jnp.zeros((devices, capacity), jnp.float32).at[home_dev, slot_index].set(-resid)
    )
    returned = lax.all_to_all(backward_slots, "shard", split_axis=0, concat_axis=0, tiled=True)
    dscore = jax.ops.segment_sum(returned.reshape(-1), wanted_rows, num_segments=local_rows)
    dscore = dscore + jax.ops.segment_sum(resid, pair_left, num_segments=local_rows)
    _, pull = jax.vjp(activate, pre)
    dpre32 = pull(dscore[:, None] * w_out.astype(jnp.float32)[None, :])[0]
    dpre = dpre32.astype(jnp.bfloat16)
    grad_bias = jnp.sum(dpre32, axis=0)
    grad_score = jnp.dot(
        dscore, hidden, precision=lax.Precision.HIGHEST, preferred_element_type=jnp.float32
    )
    term_head = jnp.stack([grad_bias, grad_score], axis=1)
    term_weight = lax.dot_general(
        embeddings, dpre, (((0,), (0,)), ((), ())), preferred_element_type=jnp.float32
    )
    return (
        lax.psum_scatter(term_weight, "shard", scatter_dimension=0, tiled=True),
        lax.psum_scatter(term_head, "shard", scatter_dimension=0, tiled=True),
    )


def per_device(embeddings, w_in, bias, w_out, pair_left, pair_home, pair_remote, outcome):
    rows = embeddings.shape[0]
    depth, units = w_in.shape
    n = lax.axis_size("shard")
    small = (
        n & (n - 1) == 0
        and 2 <= n
        and n * rows <= 2048
        and rows % LANES == 0
        and 2 * rows <= 8 * LANES
        and depth % 16 == 0
        and units % (2 * LANES) == 0
        and pair_left.shape[0] % (16 * LANES) == 0
        and pair_left.shape[0] <= 128 * LANES
        and rows <= 256
    )
    if not small:
        return by_collectives(
            embeddings, w_in, bias, w_out, pair_left, pair_home, pair_remote, outcome
        )
    return by_ppermute(
        embeddings, w_in, bias, w_out, pair_left, pair_home, pair_remote, outcome
    )


def solution(mesh):
    in_specs = (
        P("shard", None),
        P("shard", "grp"),
        P("grp"),
        P("grp"),
        P("shard"),
        P("shard", None),
        P("shard"),
        P("shard"),
    )
    out_specs = (P("shard", "grp"), P(("grp", "shard"), None))
    return jax.shard_map(
        per_device, mesh=mesh, in_specs=in_specs, out_specs=out_specs, check_vma=False
    )
```

```python
import functools

import jax
import jax.numpy as jnp
from jax import lax
from jax.experimental import pallas as pl
from jax.experimental.pallas import tpu as pltpu
from jax.sharding import PartitionSpec as P


F32 = jnp.float32
BF16 = jnp.bfloat16
LANES = 128
TAIL = 8
NT = (((1,), (1,)), ((), ()))


def activate(values):
    return jax.nn.gelu(values, approximate=True)


def vmem():
    return pl.BlockSpec(memory_space=pltpu.VMEM)


def call(body, inputs, outputs, scratch=(), flops=0, space=pltpu.VMEM):
    return pl.pallas_call(
        body,
        out_shape=outputs,
        in_specs=[pl.BlockSpec(memory_space=space)] * len(inputs),
        out_specs=[vmem()] * len(outputs),
        scratch_shapes=scratch,
        cost_estimate=pl.CostEstimate(flops=flops, bytes_accessed=1 << 20, transcendentals=0),
        compiler_params=pltpu.CompilerParams(vmem_limit_bytes=24 << 20),
    )(*inputs)


def pair_rows(ref, part, chunk):
    return ref[part, pl.ds(chunk, 1), :].astype(jnp.int32)


def transpose_kernel(own, partner, out):
    core = lax.axis_index("shard") % 2
    rows = own.shape[0]
    for j, ref in enumerate((own, partner)):
        at = pl.multiple_of((core ^ j) * rows, rows)
        out[:, pl.ds(at, rows)] = ref[...].T


def count_kernel(*refs):
    lists, (out, lefts) = refs[:-2], refs[-2:]
    own = lists[0]
    shard = lax.axis_index("shard")
    rows = out.shape[0]
    chunks = own.shape[1]
    ids = lax.broadcasted_iota(jnp.int32, (rows, LANES), 0).astype(BF16)
    nought = jnp.zeros((), BF16)

    def table(ref, home=None, sums=False):
        columns, added = [], jnp.zeros((rows, LANES), BF16)
        for q in range(chunks):
            row = pair_rows(ref, 0, q)
            if home is not None:
                row = jnp.where(pair_rows(ref, 1, q) == home, pair_rows(ref, 2, q), -1)
            hit = ids == row.astype(BF16)
            columns.append(jnp.where(hit, jnp.ones((), BF16), nought).astype(jnp.float8_e5m2))
            if sums:
                half = jnp.where(pair_rows(ref, 3, q) == 1, -0.5, 0.5).astype(BF16)
                added = added + jnp.where(hit, half, nought)
        return jnp.concatenate(columns, axis=1), added.astype(F32)

    lefts[...], total = table(own, sums=True)
    for m, ref in enumerate(lists):
        owner = shard ^ m
        here, _ = table(own, home=owner)
        there, added = table(ref, home=shard, sums=True)
        theirs, _ = table(ref)
        total = total - added
        out[:, pl.ds(pl.multiple_of(owner * rows, rows), rows)] = 0.5 * (
            lax.dot_general(lefts[...], here, NT, preferred_element_type=F32)
            + lax.dot_general(there, theirs, NT, preferred_element_type=F32)
        )
    out[:, len(lists) * rows :] = total


def forward_kernel(*refs):
    own, partner, bias, w_out = refs[:4]
    score, hidden, slope, gathered = refs[-4:]
    blocks = refs[4:-4]
    shard = lax.axis_index("shard")
    core = shard % 2
    rows = own.shape[0]
    depth = blocks[0].shape[0]
    half = hidden.shape[1]
    lane = pl.multiple_of(core * half, half)
    for m, ref in enumerate(blocks):
        at = pl.multiple_of((shard ^ m) * depth, depth)
        gathered[pl.ds(at, depth), :] = ref[:, pl.ds(lane, half)]
    shift = bias[:, pl.ds(lane, half)].astype(F32)
    weights = w_out[:, pl.ds(lane, half)]
    for j, ref in enumerate((own, partner)):
        at = pl.multiple_of((core ^ j) * rows, rows)
        pre = jnp.dot(ref[...], gathered[...], preferred_element_type=F32) + shift
        square = pre * pre
        scale = 0.7978845608028654
        t = jnp.tanh(scale * (pre + 0.044715 * (square * pre)))
        out = (pre * (0.5 * (1.0 + t))).astype(BF16)
        hidden[pl.ds(at, rows), :] = out
        slope[pl.ds(at, rows), :] = 0.5 * (1.0 + t) + (0.5 * pre) * (1.0 - t * t) * (
            scale * (1.0 + (3.0 * 0.044715) * square)
        )
        part = lax.dot_general(
            jnp.broadcast_to(weights, (8, half)), out, NT, preferred_element_type=F32
        )
        tiles = rows // LANES
        for q in range(tiles):
            piece = jnp.broadcast_to(part[0:1, q * LANES : (q + 1) * LANES], (score.shape[0], LANES))
            score[:, pl.ds((core ^ j) * tiles + q, 1), :] = piece.reshape(score.shape[0], 1, LANES)


def exponent_of(largest, limit):
    return jnp.maximum(jnp.ceil(jnp.log2(jnp.maximum(largest, 1e-30) * (1.0 / limit))), -100.0)


def coded(values):
    power = exponent_of(jnp.abs(values), 16000.0)
    scaled = values * jnp.exp2(-power)
    high = jnp.round(scaled)
    low = jnp.round((scaled - high) * 32000.0)
    return [power, high, low]


def decoded(rows, at):
    return (rows[at + 1 : at + 2, :] + rows[at + 2 : at + 3, :] * (1.0 / 32000.0)) * jnp.exp2(rows[at : at + 1, :])


def pair_kernel(groups, received, counts, dscore):
    shard = lax.axis_index("shard")
    rows = counts.shape[0]
    n = (counts.shape[1] - LANES) // rows
    tiles = rows // LANES

    def scores_of(s):
        z, j = s // 2, s % 2
        parts = [
            received[g * n + 2 * z + k, pl.ds(j * tiles, tiles), :] for g in range(groups) for k in range(2)
        ]
        while len(parts) > 1:
            parts = [a + b for a, b in zip(parts[::2], parts[1::2])]
        return parts[0] * 0.5

    across = [scores_of(s) for s in range(n)]
    turned = jnp.concatenate([scores_of(shard), jnp.zeros((8 - tiles, LANES), F32)], axis=0).T
    for q in range(tiles):
        span = slice(q * LANES, (q + 1) * LANES)
        column = jnp.broadcast_to(turned[:, q : q + 1], (LANES, LANES))
        total = counts[span, n * rows :]
        for s in range(n):
            for p in range(tiles):
                at = (s * tiles + p) * LANES
                total = total + counts[span, at : at + LANES] * jnp.tanh(column - across[s][p : p + 1, :])
        dscore[span, :] = jnp.sum(total, axis=1, keepdims=True)


def dpre_of(dscores, rows_at, hidden, slope, weights, sent):
    half = hidden.shape[1]
    bias_sum, score_sum = jnp.zeros((1, half), F32), jnp.zeros((1, half), F32)
    for r in range(dscores.shape[0] // LANES):
        span = slice(r * LANES, (r + 1) * LANES)
        there = pl.ds(pl.multiple_of(rows_at + r * LANES, LANES), LANES)
        dscore = dscores[span, :]
        dpre = (dscore * weights) * slope[there, :]
        bias_sum = bias_sum + jnp.sum(dpre, axis=0, keepdims=True)
        score_sum = score_sum + jnp.sum(dscore * hidden[there, :].astype(F32), axis=0, keepdims=True)
        sent[span, :] = dpre.astype(BF16)
    return jnp.concatenate([bias_sum, score_sum], axis=0)


def weights_of(w_out, half):
    core = lax.axis_index("shard") % 2
    return w_out[:, pl.ds(pl.multiple_of(core * half, half), half)].astype(F32)


def own_kernel(dscores, flipped, hidden, slope, w_out, terms, sums, sent):
    core = lax.axis_index("shard") % 2
    rows = dscores.shape[0]
    at = pl.multiple_of(core * rows, rows)
    sums[...] = dpre_of(dscores, at, hidden, slope, weights_of(w_out, hidden.shape[1]), sent)
    terms[...] = jnp.dot(flipped[:, pl.ds(at, rows)], sent[...], preferred_element_type=F32)


def block_of(m, flipped, own_terms, sent, depth):
    shard = lax.axis_index("shard")
    rows = sent.shape[0]
    at = pl.ds(pl.multiple_of((shard ^ m) * depth, depth), depth)
    columns = pl.ds(pl.multiple_of((1 - shard % 2) * rows, rows), rows)
    return own_terms[at, :] + jnp.dot(flipped[at, columns], sent[...], preferred_element_type=F32)


def write_message(ref, block, heads):
    depth, half = block.shape
    extra = coded(heads[0:1, :]) + coded(heads[1:2, :])
    power = exponent_of(jnp.max(jnp.abs(block), axis=0, keepdims=True), 32000.0)
    ref[:depth, :] = jnp.round(block * jnp.exp2(-power)).astype(jnp.int32).astype(jnp.int16)
    pad = jnp.zeros((TAIL - 1 - len(extra), half), F32)
    tail = jnp.concatenate([power] + extra + [pad], axis=0)
    ref[depth:, :] = tail.astype(jnp.int32).astype(jnp.int16)


def far_kernel(first, dscores, own_terms, own_sums, flipped, hidden, slope, w_out, heads, sent, *messages):
    core = lax.axis_index("shard") % 2
    at = (1 - core) * dscores.shape[0]
    sums = dpre_of(dscores, at, hidden, slope, weights_of(w_out, hidden.shape[1]), sent)
    heads[...] = own_sums[...] + sums
    for m, ref in enumerate(messages, first):
        write_message(ref, block_of(m, flipped, own_terms, sent, ref.shape[0] - TAIL), heads[...])


def near_kernel(heads, sent, own_terms, flipped, kept, *messages):
    kept[...] = block_of(0, flipped, own_terms, sent, kept.shape[0])
    for m, ref in enumerate(messages, 1):
        write_message(ref, block_of(m, flipped, own_terms, sent, kept.shape[0]), heads[...])


def added(first, sums, tops, messages):
    for m, ref in enumerate(messages, first):
        depth = ref.shape[0] - TAIL
        tail = ref[depth:, :].astype(jnp.int32).astype(F32)
        sums[m % 2] = sums[m % 2] + ref[:depth, :].astype(jnp.int32).astype(F32) * jnp.exp2(tail[0:1, :])
        tops[m % 2] = tops[m % 2] + jnp.concatenate([decoded(tail, 1), decoded(tail, 4)], axis=0)


def first_sum_kernel(kept, heads, *refs):
    messages, (sums_out, tops_out) = refs[:-2], refs[-2:]
    sums = [kept[...], jnp.zeros_like(kept)]
    tops = [heads[...], jnp.zeros_like(heads)]
    added(1, sums, tops, messages)
    for k in range(2):
        sums_out[k] = sums[k]
        tops_out[k] = tops[k]


def last_sum_kernel(first, sums_in, tops_in, *refs):
    messages, (weight, head) = refs[:-2], refs[-2:]
    shard = lax.axis_index("shard")
    core = shard % 2
    half = sums_in.shape[2]
    sums = [sums_in[k] for k in range(2)]
    tops = [tops_in[k] for k in range(2)]
    added(first, sums, tops, messages)
    weight[:, pl.ds(pl.multiple_of(core * half, half), half)] = sums[0]
    weight[:, pl.ds(pl.multiple_of((1 - core) * half, half), half)] = sums[1]
    units = head.shape[1]
    start = shard * units
    chosen = jnp.where(start // half == core, tops[0], tops[1])
    chosen = jnp.concatenate([chosen, jnp.zeros((6, half), F32)], axis=0)
    head[...] = pltpu.roll(chosen, (half - start % half) % half, 1)[:2, :units]


def by_ppermute(embeddings, w_in, bias, w_out, pair_left, pair_home, pair_remote, outcome):
    rows, channels = embeddings.shape
    depth, hidden_units = w_in.shape
    half = hidden_units // 2
    n = lax.axis_size("shard")
    groups = lax.axis_size("grp")
    pair_count = pair_left.shape[0]
    chunks = pair_count // LANES

    def swap(value, m):
        return lax.ppermute(value, "shard", [(i, i ^ m) for i in range(n)])

    far = range(n - 2, 0, -2)

    def spread(value):
        got = {0: value}
        for m in far:
            got[m] = swap(value, m)
        for m in (0, *far):
            got[m + 1] = swap(got[m], 1)
        return [got[m] for m in range(n)]

    blocks = spread(w_in)
    tile = (1, chunks, LANES)
    columns = [a.reshape(tile) for a in (pair_left, pair_home, pair_remote, outcome)]
    part = lax.broadcasted_iota(jnp.int32, (4, chunks, LANES), 0)
    pairs = columns[3]
    for k in (2, 1, 0):
        pairs = jnp.where(part == k, columns[k], pairs)
    pairs = pairs.astype(jnp.int16)
    lists = spread(pairs)
    partner = swap(embeddings, 1)
    shape = jax.ShapeDtypeStruct
    (flipped,) = call(transpose_kernel, (embeddings, partner), [shape((channels, 2 * rows), BF16)])
    (counts,) = call(
        count_kernel,
        lists,
        [shape((rows, n * rows + LANES), F32)],
        [pltpu.VMEM((rows, pair_count), jnp.float8_e5m2)],
        flops=4 * rows * n * rows * pair_count,
    )
    bias, w_out = bias.reshape(1, -1), w_out.reshape(1, -1)
    score, hidden, slope = call(
        forward_kernel,
        (embeddings, partner, bias, w_out, *blocks),
        [
            shape((groups * n, 2 * rows // LANES, LANES), F32),
            shape((2 * rows, half), BF16),
            shape((2 * rows, half), F32),
        ],
        [pltpu.VMEM((channels, half), BF16)],
        flops=4 * rows * channels * half,
    )
    received = lax.all_to_all(score, ("grp", "shard"), 0, 0, tiled=True)
    (near,) = call(
        functools.partial(pair_kernel, groups), (received, counts), [shape((rows, 1), F32)], flops=rows * n * rows
    )
    next_to = swap(near, 1)
    message = shape((depth + TAIL, half), jnp.int16)
    first = n // 2
    own_terms, own_sums = call(
        own_kernel,
        (near, flipped, hidden, slope, w_out),
        [shape((channels, half), F32), shape((2, half), F32)],
        [pltpu.VMEM((rows, half), BF16)],
        flops=2 * rows * channels * half,
    )
    heads, sent, *distant = call(
        functools.partial(far_kernel, first),
        (next_to, own_terms, own_sums, flipped, hidden, slope, w_out),
        [shape((2, half), F32), shape((rows, half), BF16)] + [message] * (n - first),
        flops=rows * channels * half,
    )
    kept, *close = call(
        near_kernel,
        (heads, sent, own_terms, flipped),
        [shape((depth, half), F32)] + [message] * (first - 1),
        flops=rows * channels * half,
    )
    messages = dict(enumerate(close + distant, 1))
    got = {m: swap(messages[m], m) for m in range(n - 1, 0, -1)}
    sums, tops = call(
        first_sum_kernel,
        (kept, heads, *[got[m] for m in range(1, first)]),
        [shape((2, depth, half), F32), shape((2, 2, half), F32)],
    )
    weight, head = call(
        functools.partial(last_sum_kernel, first),
        (sums, tops, *[got[m] for m in range(first, n)]),
        [shape((depth, hidden_units), F32), shape((2, hidden_units // n), F32)],
    )
    return weight, head.T


def by_collectives(embeddings, w_in, bias, w_out, pair_left, pair_home, pair_remote, outcome):
    local_rows = embeddings.shape[0]
    devices = lax.axis_size("shard")
    pair_count = pair_left.shape[0]
    capacity = 2 * pair_count // devices
    pre = jnp.dot(
        embeddings,
        lax.all_gather(w_in, "shard", axis=0, tiled=True),
        preferred_element_type=jnp.float32,
    )
    pre = pre + bias.astype(jnp.float32)[None, :]
    hidden = activate(pre).astype(jnp.bfloat16)
    part_score = jnp.dot(hidden, w_out, preferred_element_type=jnp.float32)
    score = lax.psum(part_score, "grp")
    home_dev = pair_home[:, 0]
    onehot = (home_dev[:, None] == jnp.arange(devices, dtype=jnp.int32)[None, :]).astype(jnp.int32)
    slot_index = jnp.sum(jnp.cumsum(onehot, axis=0) * onehot, axis=1) - 1
    request = jnp.zeros((devices, capacity), jnp.int32).at[home_dev, slot_index].set(pair_remote)
    wanted = lax.all_to_all(request, "shard", split_axis=0, concat_axis=0, tiled=True)
    wanted_rows = wanted.reshape(-1)
    outgoing = score[wanted_rows].reshape(devices, capacity)
    remote_score = lax.all_to_all(outgoing, "shard", split_axis=0, concat_axis=0, tiled=True)
    margin = score[pair_left] - remote_score[home_dev, slot_index]
    resid = jax.nn.sigmoid(margin) - outcome.astype(jnp.float32)
    backward_slots = (
        jnp.zeros((devices, capacity), jnp.float32).at[home_dev, slot_index].set(-resid)
    )
    returned = lax.all_to_all(backward_slots, "shard", split_axis=0, concat_axis=0, tiled=True)
    dscore = jax.ops.segment_sum(returned.reshape(-1), wanted_rows, num_segments=local_rows)
    dscore = dscore + jax.ops.segment_sum(resid, pair_left, num_segments=local_rows)
    _, pull = jax.vjp(activate, pre)
    dpre32 = pull(dscore[:, None] * w_out.astype(jnp.float32)[None, :])[0]
    dpre = dpre32.astype(jnp.bfloat16)
    grad_bias = jnp.sum(dpre32, axis=0)
    grad_score = jnp.dot(
        dscore, hidden, precision=lax.Precision.HIGHEST, preferred_element_type=jnp.float32
    )
    term_head = jnp.stack([grad_bias, grad_score], axis=1)
    term_weight = lax.dot_general(
        embeddings, dpre, (((0,), (0,)), ((), ())), preferred_element_type=jnp.float32
    )
    return (
        lax.psum_scatter(term_weight, "shard", scatter_dimension=0, tiled=True),
        lax.psum_scatter(term_head, "shard", scatter_dimension=0, tiled=True),
    )


def per_device(embeddings, w_in, bias, w_out, pair_left, pair_home, pair_remote, outcome):
    rows = embeddings.shape[0]
    depth, units = w_in.shape
    n = lax.axis_size("shard")
    small = (
        n & (n - 1) == 0
        and 4 <= n
        and n * rows <= 2048
        and rows % LANES == 0
        and 2 * rows <= 8 * LANES
        and depth % 16 == 0
        and units % (2 * LANES) == 0
        and pair_left.shape[0] % (16 * LANES) == 0
        and pair_left.shape[0] <= 128 * LANES
        and rows <= 256
    )
    if not small:
        return by_collectives(
            embeddings, w_in, bias, w_out, pair_left, pair_home, pair_remote, outcome
        )
    return by_ppermute(
        embeddings, w_in, bias, w_out, pair_left, pair_home, pair_remote, outcome
    )


def solution(mesh):
    in_specs = (
        P("shard", None),
        P("shard", "grp"),
        P("grp"),
        P("grp"),
        P("shard"),
        P("shard", None),
        P("shard"),
        P("shard"),
    )
    out_specs = (P("shard", "grp"), P(("grp", "shard"), None))
    return jax.shard_map(
        per_device, mesh=mesh, in_specs=in_specs, out_specs=out_specs, check_vma=False
    )
```

```python
import functools

import jax
import jax.numpy as jnp
from jax import lax
from jax.experimental import pallas as pl
from jax.experimental.pallas import tpu as pltpu
from jax.sharding import PartitionSpec as P


F32 = jnp.float32
BF16 = jnp.bfloat16
LANES = 128
TAIL = 8
NT = (((1,), (1,)), ((), ()))


def activate(values):
    return jax.nn.gelu(values, approximate=True)


def vmem():
    return pl.BlockSpec(memory_space=pltpu.VMEM)


def call(body, inputs, outputs, scratch=(), flops=0, space=pltpu.VMEM):
    return pl.pallas_call(
        body,
        out_shape=outputs,
        in_specs=[pl.BlockSpec(memory_space=space)] * len(inputs),
        out_specs=[vmem()] * len(outputs),
        scratch_shapes=scratch,
        cost_estimate=pl.CostEstimate(flops=flops, bytes_accessed=1 << 20, transcendentals=0),
        compiler_params=pltpu.CompilerParams(vmem_limit_bytes=24 << 20),
    )(*inputs)


def pair_rows(ref, part, chunk):
    return ref[part, pl.ds(chunk, 1), :].astype(jnp.int32)


def transpose_kernel(own, partner, out):
    core = lax.axis_index("shard") % 2
    rows = own.shape[0]
    for j, ref in enumerate((own, partner)):
        at = pl.multiple_of((core ^ j) * rows, rows)
        out[:, pl.ds(at, rows)] = ref[...].T


def count_kernel(*refs):
    lists, (out, lefts) = refs[:-2], refs[-2:]
    own = lists[0]
    shard = lax.axis_index("shard")
    rows = out.shape[0]
    chunks = own.shape[1]
    ids = lax.broadcasted_iota(jnp.int32, (rows, LANES), 0).astype(BF16)
    nought = jnp.zeros((), BF16)

    def table(ref, home=None, sums=False):
        columns, added = [], jnp.zeros((rows, LANES), BF16)
        for q in range(chunks):
            row = pair_rows(ref, 0, q)
            if home is not None:
                row = jnp.where(pair_rows(ref, 1, q) == home, pair_rows(ref, 2, q), -1)
            hit = ids == row.astype(BF16)
            columns.append(jnp.where(hit, jnp.ones((), BF16), nought).astype(jnp.float8_e5m2))
            if sums:
                half = jnp.where(pair_rows(ref, 3, q) == 1, -0.5, 0.5).astype(BF16)
                added = added + jnp.where(hit, half, nought)
        return jnp.concatenate(columns, axis=1), added.astype(F32)

    lefts[...], total = table(own, sums=True)
    for m, ref in enumerate(lists):
        owner = shard ^ m
        here, _ = table(own, home=owner)
        there, added = table(ref, home=shard, sums=True)
        theirs, _ = table(ref)
        total = total - added
        out[:, pl.ds(pl.multiple_of(owner * rows, rows), rows)] = 0.5 * (
            lax.dot_general(lefts[...], here, NT, preferred_element_type=F32)
            + lax.dot_general(there, theirs, NT, preferred_element_type=F32)
        )
    out[:, len(lists) * rows :] = total


def late_window(depth):
    return -(-(2 * depth + LANES // 2) // LANES) * LANES


def begin_kernel(late, own, partner, *refs):
    blocks, (out, gathered) = refs[:-2], refs[-2:]
    shard = lax.axis_index("shard")
    core = shard % 2
    rows = own.shape[0]
    depth = blocks[0].shape[0]
    half = out.shape[1]
    lane = pl.multiple_of(core * half, half)
    n = len(blocks) + 2
    for m, ref in zip((m for m in range(n) if m not in (late, late + 1)), blocks):
        gathered[pl.ds(pl.multiple_of((shard ^ m) * depth, depth), depth), :] = ref[:, pl.ds(lane, half)]
    chip = (shard ^ late) // 2
    gathered[pl.ds(pl.multiple_of(chip * 2 * depth, 2 * depth), 2 * depth), :] = jnp.zeros((2 * depth, half), BF16)
    for j, ref in enumerate((own, partner)):
        at = pl.multiple_of((core ^ j) * rows, rows)
        out[pl.ds(at, rows), :] = jnp.dot(ref[...], gathered[...], preferred_element_type=F32)


def forward_kernel(late, own, partner, bias, w_out, begun, same, other, score, hidden, slope, gathered):
    shard = lax.axis_index("shard")
    core = shard % 2
    rows = own.shape[0]
    depth = same.shape[0]
    half = hidden.shape[1]
    lane = pl.multiple_of(core * half, half)
    window = gathered.shape[0]
    first = (shard ^ late) // 2 * (2 * depth)
    tile = pl.multiple_of(first // LANES * LANES, LANES)
    gathered[...] = jnp.zeros_like(gathered)
    for k, ref in ((core, same), (1 - core, other)):
        at = pl.multiple_of(first % LANES + k * depth, 16)
        gathered[pl.ds(at, depth), :] = ref[:, pl.ds(lane, half)]
    shift = bias[:, pl.ds(lane, half)].astype(F32)
    weights = w_out[:, pl.ds(lane, half)]
    for j, ref in enumerate((own, partner)):
        at = pl.multiple_of((core ^ j) * rows, rows)
        late_part = jnp.dot(ref[:, pl.ds(tile, window)], gathered[...], preferred_element_type=F32)
        pre = (begun[pl.ds(at, rows), :] + late_part) + shift
        square = pre * pre
        scale = 0.7978845608028654
        t = jnp.tanh(scale * (pre + 0.044715 * (square * pre)))
        out = (pre * (0.5 * (1.0 + t))).astype(BF16)
        hidden[pl.ds(at, rows), :] = out
        slope[pl.ds(at, rows), :] = 0.5 * (1.0 + t) + (0.5 * pre) * (1.0 - t * t) * (
            scale * (1.0 + (3.0 * 0.044715) * square)
        )
        part = lax.dot_general(
            jnp.broadcast_to(weights, (8, half)), out, NT, preferred_element_type=F32
        )
        tiles = rows // LANES
        for q in range(tiles):
            piece = jnp.broadcast_to(part[0:1, q * LANES : (q + 1) * LANES], (score.shape[0], LANES))
            score[:, pl.ds((core ^ j) * tiles + q, 1), :] = piece.reshape(score.shape[0], 1, LANES)


def exponent_of(largest, limit):
    return jnp.maximum(jnp.ceil(jnp.log2(jnp.maximum(largest, 1e-30) * (1.0 / limit))), -100.0)


def coded(values):
    power = exponent_of(jnp.abs(values), 16000.0)
    scaled = values * jnp.exp2(-power)
    high = jnp.round(scaled)
    low = jnp.round((scaled - high) * 32000.0)
    return [power, high, low]


def decoded(rows, at):
    return (rows[at + 1 : at + 2, :] + rows[at + 2 : at + 3, :] * (1.0 / 32000.0)) * jnp.exp2(rows[at : at + 1, :])


def pair_kernel(groups, received, counts, dscore):
    shard = lax.axis_index("shard")
    rows = counts.shape[0]
    n = (counts.shape[1] - LANES) // rows
    tiles = rows // LANES

    def scores_of(s):
        z, j = s // 2, s % 2
        parts = [
            received[g * n + 2 * z + k, pl.ds(j * tiles, tiles), :] for g in range(groups) for k in range(2)
        ]
        while len(parts) > 1:
            parts = [a + b for a, b in zip(parts[::2], parts[1::2])]
        return parts[0] * 0.5

    across = [scores_of(s) for s in range(n)]
    turned = jnp.concatenate([scores_of(shard), jnp.zeros((8 - tiles, LANES), F32)], axis=0).T
    for q in range(tiles):
        span = slice(q * LANES, (q + 1) * LANES)
        column = jnp.broadcast_to(turned[:, q : q + 1], (LANES, LANES))
        total = counts[span, n * rows :]
        for s in range(n):
            for p in range(tiles):
                at = (s * tiles + p) * LANES
                total = total + counts[span, at : at + LANES] * jnp.tanh(column - across[s][p : p + 1, :])
        dscore[span, :] = jnp.sum(total, axis=1, keepdims=True)


def dpre_of(dscores, rows_at, hidden, slope, weights, sent):
    half = hidden.shape[1]
    bias_sum, score_sum = jnp.zeros((1, half), F32), jnp.zeros((1, half), F32)
    for r in range(dscores.shape[0] // LANES):
        span = slice(r * LANES, (r + 1) * LANES)
        there = pl.ds(pl.multiple_of(rows_at + r * LANES, LANES), LANES)
        dscore = dscores[span, :]
        dpre = (dscore * weights) * slope[there, :]
        bias_sum = bias_sum + jnp.sum(dpre, axis=0, keepdims=True)
        score_sum = score_sum + jnp.sum(dscore * hidden[there, :].astype(F32), axis=0, keepdims=True)
        sent[span, :] = dpre.astype(BF16)
    return jnp.concatenate([bias_sum, score_sum], axis=0)


def weights_of(w_out, half):
    core = lax.axis_index("shard") % 2
    return w_out[:, pl.ds(pl.multiple_of(core * half, half), half)].astype(F32)


def own_kernel(dscores, flipped, hidden, slope, w_out, terms, sums, sent):
    core = lax.axis_index("shard") % 2
    rows = dscores.shape[0]
    at = pl.multiple_of(core * rows, rows)
    sums[...] = dpre_of(dscores, at, hidden, slope, weights_of(w_out, hidden.shape[1]), sent)
    terms[...] = jnp.dot(flipped[:, pl.ds(at, rows)], sent[...], preferred_element_type=F32)


def block_of(m, flipped, own_terms, sent, depth):
    shard = lax.axis_index("shard")
    rows = sent.shape[0]
    at = pl.ds(pl.multiple_of((shard ^ m) * depth, depth), depth)
    columns = pl.ds(pl.multiple_of((1 - shard % 2) * rows, rows), rows)
    return own_terms[at, :] + jnp.dot(flipped[at, columns], sent[...], preferred_element_type=F32)


def write_message(ref, block, heads):
    depth, half = block.shape
    extra = coded(heads[0:1, :]) + coded(heads[1:2, :])
    power = exponent_of(jnp.max(jnp.abs(block), axis=0, keepdims=True), 32000.0)
    ref[:depth, :] = jnp.round(block * jnp.exp2(-power)).astype(jnp.int32).astype(jnp.int16)
    pad = jnp.zeros((TAIL - 1 - len(extra), half), F32)
    tail = jnp.concatenate([power] + extra + [pad], axis=0)
    ref[depth:, :] = tail.astype(jnp.int32).astype(jnp.int16)


def far_kernel(first, dscores, own_terms, own_sums, flipped, hidden, slope, w_out, heads, sent, *messages):
    core = lax.axis_index("shard") % 2
    at = (1 - core) * dscores.shape[0]
    sums = dpre_of(dscores, at, hidden, slope, weights_of(w_out, hidden.shape[1]), sent)
    heads[...] = own_sums[...] + sums
    for m, ref in enumerate(messages, first):
        write_message(ref, block_of(m, flipped, own_terms, sent, ref.shape[0] - TAIL), heads[...])


def near_kernel(heads, sent, own_terms, flipped, kept, *messages):
    kept[...] = block_of(0, flipped, own_terms, sent, kept.shape[0])
    for m, ref in enumerate(messages, 1):
        write_message(ref, block_of(m, flipped, own_terms, sent, kept.shape[0]), heads[...])


def added(first, sums, tops, messages):
    for m, ref in enumerate(messages, first):
        depth = ref.shape[0] - TAIL
        tail = ref[depth:, :].astype(jnp.int32).astype(F32)
        sums[m % 2] = sums[m % 2] + ref[:depth, :].astype(jnp.int32).astype(F32) * jnp.exp2(tail[0:1, :])
        tops[m % 2] = tops[m % 2] + jnp.concatenate([decoded(tail, 1), decoded(tail, 4)], axis=0)


def first_sum_kernel(kept, heads, *refs):
    messages, (sums_out, tops_out) = refs[:-2], refs[-2:]
    sums = [kept[...], jnp.zeros_like(kept)]
    tops = [heads[...], jnp.zeros_like(heads)]
    added(1, sums, tops, messages)
    for k in range(2):
        sums_out[k] = sums[k]
        tops_out[k] = tops[k]


def last_sum_kernel(first, sums_in, tops_in, *refs):
    messages, (weight, head) = refs[:-2], refs[-2:]
    shard = lax.axis_index("shard")
    core = shard % 2
    half = sums_in.shape[2]
    sums = [sums_in[k] for k in range(2)]
    tops = [tops_in[k] for k in range(2)]
    added(first, sums, tops, messages)
    weight[:, pl.ds(pl.multiple_of(core * half, half), half)] = sums[0]
    weight[:, pl.ds(pl.multiple_of((1 - core) * half, half), half)] = sums[1]
    units = head.shape[1]
    start = shard * units
    chosen = jnp.where(start // half == core, tops[0], tops[1])
    chosen = jnp.concatenate([chosen, jnp.zeros((6, half), F32)], axis=0)
    head[...] = pltpu.roll(chosen, (half - start % half) % half, 1)[:2, :units]


def by_ppermute(embeddings, w_in, bias, w_out, pair_left, pair_home, pair_remote, outcome):
    rows, channels = embeddings.shape
    depth, hidden_units = w_in.shape
    half = hidden_units // 2
    n = lax.axis_size("shard")
    groups = lax.axis_size("grp")
    pair_count = pair_left.shape[0]
    chunks = pair_count // LANES

    def swap(value, m):
        return lax.ppermute(value, "shard", [(i, i ^ m) for i in range(n)])

    far = range(n - 2, 0, -2)

    def spread(value):
        got = {0: value}
        for m in far:
            got[m] = swap(value, m)
        for m in (0, *far):
            got[m + 1] = swap(got[m], 1)
        return [got[m] for m in range(n)]

    blocks = spread(w_in)
    tile = (1, chunks, LANES)
    columns = [a.reshape(tile) for a in (pair_left, pair_home, pair_remote, outcome)]
    part = lax.broadcasted_iota(jnp.int32, (4, chunks, LANES), 0)
    pairs = columns[3]
    for k in (2, 1, 0):
        pairs = jnp.where(part == k, columns[k], pairs)
    pairs = pairs.astype(jnp.int16)
    lists = spread(pairs)
    partner = swap(embeddings, 1)
    shape = jax.ShapeDtypeStruct
    (flipped,) = call(transpose_kernel, (embeddings, partner), [shape((channels, 2 * rows), BF16)])
    (counts,) = call(
        count_kernel,
        lists,
        [shape((rows, n * rows + LANES), F32)],
        [pltpu.VMEM((rows, pair_count), jnp.float8_e5m2)],
        flops=4 * rows * n * rows * pair_count,
    )
    bias, w_out = bias.reshape(1, -1), w_out.reshape(1, -1)
    late = n // 2
    (begun,) = call(
        functools.partial(begin_kernel, late),
        (embeddings, partner, *[blocks[m] for m in range(n) if m not in (late, late + 1)]),
        [shape((2 * rows, half), F32)],
        [pltpu.VMEM((channels, half), BF16)],
        flops=3 * rows * channels * half,
    )
    score, hidden, slope = call(
        functools.partial(forward_kernel, late),
        (embeddings, partner, bias, w_out, begun, blocks[late], blocks[late + 1]),
        [
            shape((groups * n, 2 * rows // LANES, LANES), F32),
            shape((2 * rows, half), BF16),
            shape((2 * rows, half), F32),
        ],
        [pltpu.VMEM((late_window(depth), half), BF16)],
        flops=rows * channels * half,
    )
    received = lax.all_to_all(score, ("grp", "shard"), 0, 0, tiled=True)
    (near,) = call(
        functools.partial(pair_kernel, groups), (received, counts), [shape((rows, 1), F32)], flops=rows * n * rows
    )
    next_to = swap(near, 1)
    message = shape((depth + TAIL, half), jnp.int16)
    first = n // 2
    own_terms, own_sums = call(
        own_kernel,
        (near, flipped, hidden, slope, w_out),
        [shape((channels, half), F32), shape((2, half), F32)],
        [pltpu.VMEM((rows, half), BF16)],
        flops=2 * rows * channels * half,
    )
    heads, sent, *distant = call(
        functools.partial(far_kernel, first),
        (next_to, own_terms, own_sums, flipped, hidden, slope, w_out),
        [shape((2, half), F32), shape((rows, half), BF16)] + [message] * (n - first),
        flops=rows * channels * half,
    )
    kept, *close = call(
        near_kernel,
        (heads, sent, own_terms, flipped),
        [shape((depth, half), F32)] + [message] * (first - 1),
        flops=rows * channels * half,
    )
    messages = dict(enumerate(close + distant, 1))
    got = {m: swap(messages[m], m) for m in range(n - 1, 0, -1)}
    sums, tops = call(
        first_sum_kernel,
        (kept, heads, *[got[m] for m in range(1, first)]),
        [shape((2, depth, half), F32), shape((2, 2, half), F32)],
    )
    weight, head = call(
        functools.partial(last_sum_kernel, first),
        (sums, tops, *[got[m] for m in range(first, n)]),
        [shape((depth, hidden_units), F32), shape((2, hidden_units // n), F32)],
    )
    return weight, head.T


def by_collectives(embeddings, w_in, bias, w_out, pair_left, pair_home, pair_remote, outcome):
    local_rows = embeddings.shape[0]
    devices = lax.axis_size("shard")
    pair_count = pair_left.shape[0]
    capacity = 2 * pair_count // devices
    pre = jnp.dot(
        embeddings,
        lax.all_gather(w_in, "shard", axis=0, tiled=True),
        preferred_element_type=jnp.float32,
    )
    pre = pre + bias.astype(jnp.float32)[None, :]
    hidden = activate(pre).astype(jnp.bfloat16)
    part_score = jnp.dot(hidden, w_out, preferred_element_type=jnp.float32)
    score = lax.psum(part_score, "grp")
    home_dev = pair_home[:, 0]
    onehot = (home_dev[:, None] == jnp.arange(devices, dtype=jnp.int32)[None, :]).astype(jnp.int32)
    slot_index = jnp.sum(jnp.cumsum(onehot, axis=0) * onehot, axis=1) - 1
    request = jnp.zeros((devices, capacity), jnp.int32).at[home_dev, slot_index].set(pair_remote)
    wanted = lax.all_to_all(request, "shard", split_axis=0, concat_axis=0, tiled=True)
    wanted_rows = wanted.reshape(-1)
    outgoing = score[wanted_rows].reshape(devices, capacity)
    remote_score = lax.all_to_all(outgoing, "shard", split_axis=0, concat_axis=0, tiled=True)
    margin = score[pair_left] - remote_score[home_dev, slot_index]
    resid = jax.nn.sigmoid(margin) - outcome.astype(jnp.float32)
    backward_slots = (
        jnp.zeros((devices, capacity), jnp.float32).at[home_dev, slot_index].set(-resid)
    )
    returned = lax.all_to_all(backward_slots, "shard", split_axis=0, concat_axis=0, tiled=True)
    dscore = jax.ops.segment_sum(returned.reshape(-1), wanted_rows, num_segments=local_rows)
    dscore = dscore + jax.ops.segment_sum(resid, pair_left, num_segments=local_rows)
    _, pull = jax.vjp(activate, pre)
    dpre32 = pull(dscore[:, None] * w_out.astype(jnp.float32)[None, :])[0]
    dpre = dpre32.astype(jnp.bfloat16)
    grad_bias = jnp.sum(dpre32, axis=0)
    grad_score = jnp.dot(
        dscore, hidden, precision=lax.Precision.HIGHEST, preferred_element_type=jnp.float32
    )
    term_head = jnp.stack([grad_bias, grad_score], axis=1)
    term_weight = lax.dot_general(
        embeddings, dpre, (((0,), (0,)), ((), ())), preferred_element_type=jnp.float32
    )
    return (
        lax.psum_scatter(term_weight, "shard", scatter_dimension=0, tiled=True),
        lax.psum_scatter(term_head, "shard", scatter_dimension=0, tiled=True),
    )


def per_device(embeddings, w_in, bias, w_out, pair_left, pair_home, pair_remote, outcome):
    rows = embeddings.shape[0]
    depth, units = w_in.shape
    n = lax.axis_size("shard")
    small = (
        n & (n - 1) == 0
        and 4 <= n
        and n * rows <= 2048
        and rows % LANES == 0
        and 2 * rows <= 8 * LANES
        and depth % 16 == 0
        and units % (2 * LANES) == 0
        and 2 * depth % (LANES // 2) == 0
        and embeddings.shape[1] == n * depth
        and (n - 2) * depth // LANES * LANES + late_window(depth) <= n * depth
        and pair_left.shape[0] % (16 * LANES) == 0
        and pair_left.shape[0] <= 128 * LANES
        and rows <= 256
    )
    if not small:
        return by_collectives(
            embeddings, w_in, bias, w_out, pair_left, pair_home, pair_remote, outcome
        )
    return by_ppermute(
        embeddings, w_in, bias, w_out, pair_left, pair_home, pair_remote, outcome
    )


def solution(mesh):
    in_specs = (
        P("shard", None),
        P("shard", "grp"),
        P("grp"),
        P("grp"),
        P("shard"),
        P("shard", None),
        P("shard"),
        P("shard"),
    )
    out_specs = (P("shard", "grp"), P(("grp", "shard"), None))
    return jax.shard_map(
        per_device, mesh=mesh, in_specs=in_specs, out_specs=out_specs, check_vma=False
    )
```

```python
import functools

import jax
import jax.numpy as jnp
from jax import lax
from jax.experimental import pallas as pl
from jax.experimental.pallas import tpu as pltpu
from jax.sharding import PartitionSpec as P


F32 = jnp.float32
BF16 = jnp.bfloat16
LANES = 128
TAIL = 8
SCALE = 0.7978845608028654
NT = (((1,), (1,)), ((), ()))


def activate(values):
    return jax.nn.gelu(values, approximate=True)


def vmem():
    return pl.BlockSpec(memory_space=pltpu.VMEM)


def call(body, inputs, outputs, scratch=(), flops=0, space=pltpu.VMEM):
    return pl.pallas_call(
        body,
        out_shape=outputs,
        in_specs=[pl.BlockSpec(memory_space=space)] * len(inputs),
        out_specs=[vmem()] * len(outputs),
        scratch_shapes=scratch,
        cost_estimate=pl.CostEstimate(flops=flops, bytes_accessed=1 << 20, transcendentals=0),
        compiler_params=pltpu.CompilerParams(vmem_limit_bytes=24 << 20),
    )(*inputs)


def pair_rows(ref, part, chunk):
    return ref[part, pl.ds(chunk, 1), :].astype(jnp.int32)


def transpose_kernel(own, partner, out):
    core = lax.axis_index("shard") % 2
    rows = own.shape[0]
    for j, ref in enumerate((own, partner)):
        at = pl.multiple_of((core ^ j) * rows, rows)
        out[:, pl.ds(at, rows)] = ref[...].T


def count_kernel(*refs):
    lists, (out, lefts) = refs[:-2], refs[-2:]
    own = lists[0]
    shard = lax.axis_index("shard")
    rows = out.shape[0]
    chunks = own.shape[1]
    ids = lax.broadcasted_iota(jnp.int32, (rows, LANES), 0).astype(BF16)
    nought = jnp.zeros((), BF16)

    def table(ref, home=None, sums=False):
        columns, added = [], jnp.zeros((rows, LANES), BF16)
        for q in range(chunks):
            row = pair_rows(ref, 0, q)
            if home is not None:
                row = jnp.where(pair_rows(ref, 1, q) == home, pair_rows(ref, 2, q), -1)
            hit = ids == row.astype(BF16)
            columns.append(jnp.where(hit, jnp.ones((), BF16), nought).astype(jnp.float8_e5m2))
            if sums:
                half = jnp.where(pair_rows(ref, 3, q) == 1, -0.5, 0.5).astype(BF16)
                added = added + jnp.where(hit, half, nought)
        return jnp.concatenate(columns, axis=1), added.astype(F32)

    lefts[...], total = table(own, sums=True)
    for m, ref in enumerate(lists):
        owner = shard ^ m
        here, _ = table(own, home=owner)
        there, added = table(ref, home=shard, sums=True)
        theirs, _ = table(ref)
        total = total - added
        out[:, pl.ds(pl.multiple_of(owner * rows, rows), rows)] = 0.5 * (
            lax.dot_general(lefts[...], here, NT, preferred_element_type=F32)
            + lax.dot_general(there, theirs, NT, preferred_element_type=F32)
        )
    out[:, len(lists) * rows :] = total


def late_window(depth):
    return -(-(2 * depth + LANES // 2) // LANES) * LANES


def begin_kernel(late, own, partner, *refs):
    blocks, (out, gathered) = refs[:-2], refs[-2:]
    shard = lax.axis_index("shard")
    core = shard % 2
    rows = own.shape[0]
    depth = blocks[0].shape[0]
    half = out.shape[1]
    lane = pl.multiple_of(core * half, half)
    n = len(blocks) + 2
    for m, ref in zip((m for m in range(n) if m not in (late, late + 1)), blocks):
        gathered[pl.ds(pl.multiple_of((shard ^ m) * depth, depth), depth), :] = ref[:, pl.ds(lane, half)]
    chip = (shard ^ late) // 2
    gathered[pl.ds(pl.multiple_of(chip * 2 * depth, 2 * depth), 2 * depth), :] = jnp.zeros((2 * depth, half), BF16)
    for j, ref in enumerate((own, partner)):
        at = pl.multiple_of((core ^ j) * rows, rows)
        out[pl.ds(at, rows), :] = jnp.dot(ref[...], gathered[...], preferred_element_type=F32)


def forward_kernel(late, own, partner, bias, w_out, begun, same, other, score, hidden, kept, gathered):
    shard = lax.axis_index("shard")
    core = shard % 2
    rows = own.shape[0]
    depth = same.shape[0]
    half = hidden.shape[1]
    lane = pl.multiple_of(core * half, half)
    window = gathered.shape[0]
    first = (shard ^ late) // 2 * (2 * depth)
    tile = pl.multiple_of(first // LANES * LANES, LANES)
    gathered[...] = jnp.zeros_like(gathered)
    for k, ref in ((core, same), (1 - core, other)):
        at = pl.multiple_of(first % LANES + k * depth, 16)
        gathered[pl.ds(at, depth), :] = ref[:, pl.ds(lane, half)]
    shift = bias[:, pl.ds(lane, half)].astype(F32)
    weights = w_out[:, pl.ds(lane, half)]
    for j, ref in enumerate((own, partner)):
        at = pl.multiple_of((core ^ j) * rows, rows)
        late_part = jnp.dot(ref[:, pl.ds(tile, window)], gathered[...], preferred_element_type=F32)
        pre = (begun[pl.ds(at, rows), :] + late_part) + shift
        kept[pl.ds(at, rows), :] = pre
        t = jnp.tanh(SCALE * (pre + 0.044715 * (pre * pre * pre)))
        out = (pre * (0.5 * (1.0 + t))).astype(BF16)
        hidden[pl.ds(at, rows), :] = out
        part = lax.dot_general(
            jnp.broadcast_to(weights, (8, half)), out, NT, preferred_element_type=F32
        )
        tiles = rows // LANES
        for q in range(tiles):
            piece = jnp.broadcast_to(part[0:1, q * LANES : (q + 1) * LANES], (score.shape[0], LANES))
            score[:, pl.ds((core ^ j) * tiles + q, 1), :] = piece.reshape(score.shape[0], 1, LANES)


def exponent_of(largest, limit):
    return jnp.maximum(jnp.ceil(jnp.log2(jnp.maximum(largest, 1e-30) * (1.0 / limit))), -100.0)


def coded(values):
    power = exponent_of(jnp.abs(values), 16000.0)
    scaled = values * jnp.exp2(-power)
    high = jnp.round(scaled)
    low = jnp.round((scaled - high) * 32000.0)
    return [power, high, low]


def decoded(rows, at):
    return (rows[at + 1 : at + 2, :] + rows[at + 2 : at + 3, :] * (1.0 / 32000.0)) * jnp.exp2(rows[at : at + 1, :])


def pair_kernel(groups, received, counts, dscore):
    shard = lax.axis_index("shard")
    rows = counts.shape[0]
    n = (counts.shape[1] - LANES) // rows
    tiles = rows // LANES

    def scores_of(s):
        z, j = s // 2, s % 2
        parts = [
            received[g * n + 2 * z + k, pl.ds(j * tiles, tiles), :] for g in range(groups) for k in range(2)
        ]
        while len(parts) > 1:
            parts = [a + b for a, b in zip(parts[::2], parts[1::2])]
        return parts[0] * 0.5

    across = [scores_of(s) for s in range(n)]
    turned = jnp.concatenate([scores_of(shard), jnp.zeros((8 - tiles, LANES), F32)], axis=0).T
    for q in range(tiles):
        span = slice(q * LANES, (q + 1) * LANES)
        column = jnp.broadcast_to(turned[:, q : q + 1], (LANES, LANES))
        total = counts[span, n * rows :]
        for s in range(n):
            for p in range(tiles):
                at = (s * tiles + p) * LANES
                total = total + counts[span, at : at + LANES] * jnp.tanh(column - across[s][p : p + 1, :])
        dscore[span, :] = jnp.sum(total, axis=1, keepdims=True)


def slope_of(pre):
    square = pre * pre
    t = jnp.tanh(SCALE * (pre + 0.044715 * (square * pre)))
    return 0.5 * (1.0 + t) + (0.5 * pre) * (1.0 - t * t) * (SCALE * (1.0 + (3.0 * 0.044715) * square))


def dpre_of(dscores, rows_at, hidden, slope, weights, sent):
    half = hidden.shape[1]
    bias_sum, score_sum = jnp.zeros((1, half), F32), jnp.zeros((1, half), F32)
    for r in range(dscores.shape[0] // LANES):
        span = slice(r * LANES, (r + 1) * LANES)
        there = pl.ds(pl.multiple_of(rows_at + r * LANES, LANES), LANES)
        dscore = dscores[span, :]
        dpre = (dscore * weights) * slope(span, there)
        bias_sum = bias_sum + jnp.sum(dpre, axis=0, keepdims=True)
        score_sum = score_sum + jnp.sum(dscore * hidden[there, :].astype(F32), axis=0, keepdims=True)
        sent[span, :] = dpre.astype(BF16)
    return jnp.concatenate([bias_sum, score_sum], axis=0)


def weights_of(w_out, half):
    core = lax.axis_index("shard") % 2
    return w_out[:, pl.ds(pl.multiple_of(core * half, half), half)].astype(F32)


def own_kernel(dscores, flipped, hidden, pre, w_out, terms, sums, slope, sent):
    core = lax.axis_index("shard") % 2
    rows = dscores.shape[0]
    at = pl.multiple_of(core * rows, rows)
    weights = weights_of(w_out, hidden.shape[1])
    sums[...] = dpre_of(dscores, at, hidden, lambda _, there: slope_of(pre[there, :]), weights, sent)
    slope[...] = slope_of(pre[pl.ds(pl.multiple_of((1 - core) * rows, rows), rows), :])
    terms[...] = jnp.dot(flipped[:, pl.ds(at, rows)], sent[...], preferred_element_type=F32)


def block_of(m, flipped, own_terms, sent, depth):
    shard = lax.axis_index("shard")
    rows = sent.shape[0]
    at = pl.ds(pl.multiple_of((shard ^ m) * depth, depth), depth)
    columns = pl.ds(pl.multiple_of((1 - shard % 2) * rows, rows), rows)
    return own_terms[at, :] + jnp.dot(flipped[at, columns], sent[...], preferred_element_type=F32)


def write_message(ref, block, heads):
    depth, half = block.shape
    extra = coded(heads[0:1, :]) + coded(heads[1:2, :])
    power = exponent_of(jnp.max(jnp.abs(block), axis=0, keepdims=True), 32000.0)
    ref[:depth, :] = jnp.round(block * jnp.exp2(-power)).astype(jnp.int32).astype(jnp.int16)
    pad = jnp.zeros((TAIL - 1 - len(extra), half), F32)
    tail = jnp.concatenate([power] + extra + [pad], axis=0)
    ref[depth:, :] = tail.astype(jnp.int32).astype(jnp.int16)


def far_kernel(first, dscores, own_terms, own_sums, flipped, hidden, slope, w_out, heads, sent, *messages):
    core = lax.axis_index("shard") % 2
    at = (1 - core) * dscores.shape[0]
    weights = weights_of(w_out, hidden.shape[1])
    sums = dpre_of(dscores, at, hidden, lambda span, _: slope[span, :], weights, sent)
    heads[...] = own_sums[...] + sums
    for m, ref in enumerate(messages, first):
        write_message(ref, block_of(m, flipped, own_terms, sent, ref.shape[0] - TAIL), heads[...])


def near_kernel(heads, sent, own_terms, flipped, kept, *messages):
    kept[...] = block_of(0, flipped, own_terms, sent, kept.shape[0])
    for m, ref in enumerate(messages, 1):
        write_message(ref, block_of(m, flipped, own_terms, sent, kept.shape[0]), heads[...])


def added(first, sums, tops, messages):
    for m, ref in enumerate(messages, first):
        depth = ref.shape[0] - TAIL
        tail = ref[depth:, :].astype(jnp.int32).astype(F32)
        sums[m % 2] = sums[m % 2] + ref[:depth, :].astype(jnp.int32).astype(F32) * jnp.exp2(tail[0:1, :])
        tops[m % 2] = tops[m % 2] + jnp.concatenate([decoded(tail, 1), decoded(tail, 4)], axis=0)


def first_sum_kernel(kept, heads, *refs):
    messages, (sums_out, tops_out) = refs[:-2], refs[-2:]
    sums = [kept[...], jnp.zeros_like(kept)]
    tops = [heads[...], jnp.zeros_like(heads)]
    added(1, sums, tops, messages)
    for k in range(2):
        sums_out[k] = sums[k]
        tops_out[k] = tops[k]


def last_sum_kernel(first, sums_in, tops_in, *refs):
    messages, (weight, head) = refs[:-2], refs[-2:]
    shard = lax.axis_index("shard")
    core = shard % 2
    half = sums_in.shape[2]
    sums = [sums_in[k] for k in range(2)]
    tops = [tops_in[k] for k in range(2)]
    added(first, sums, tops, messages)
    weight[:, pl.ds(pl.multiple_of(core * half, half), half)] = sums[0]
    weight[:, pl.ds(pl.multiple_of((1 - core) * half, half), half)] = sums[1]
    units = head.shape[1]
    start = shard * units
    chosen = jnp.where(start // half == core, tops[0], tops[1])
    chosen = jnp.concatenate([chosen, jnp.zeros((6, half), F32)], axis=0)
    head[...] = pltpu.roll(chosen, (half - start % half) % half, 1)[:2, :units]


def by_ppermute(embeddings, w_in, bias, w_out, pair_left, pair_home, pair_remote, outcome):
    rows, channels = embeddings.shape
    depth, hidden_units = w_in.shape
    half = hidden_units // 2
    n = lax.axis_size("shard")
    groups = lax.axis_size("grp")
    pair_count = pair_left.shape[0]
    chunks = pair_count // LANES

    def swap(value, m):
        return lax.ppermute(value, "shard", [(i, i ^ m) for i in range(n)])

    far = range(n - 2, 0, -2)

    def spread(value):
        got = {0: value}
        for m in far:
            got[m] = swap(value, m)
        for m in (0, *far):
            got[m + 1] = swap(got[m], 1)
        return [got[m] for m in range(n)]

    blocks = spread(w_in)
    tile = (1, chunks, LANES)
    columns = [a.reshape(tile) for a in (pair_left, pair_home, pair_remote, outcome)]
    part = lax.broadcasted_iota(jnp.int32, (4, chunks, LANES), 0)
    pairs = columns[3]
    for k in (2, 1, 0):
        pairs = jnp.where(part == k, columns[k], pairs)
    pairs = pairs.astype(jnp.int16)
    lists = spread(pairs)
    partner = swap(embeddings, 1)
    shape = jax.ShapeDtypeStruct
    (flipped,) = call(transpose_kernel, (embeddings, partner), [shape((channels, 2 * rows), BF16)])
    (counts,) = call(
        count_kernel,
        lists,
        [shape((rows, n * rows + LANES), F32)],
        [pltpu.VMEM((rows, pair_count), jnp.float8_e5m2)],
        flops=4 * rows * n * rows * pair_count,
    )
    bias, w_out = bias.reshape(1, -1), w_out.reshape(1, -1)
    late = n // 2
    (begun,) = call(
        functools.partial(begin_kernel, late),
        (embeddings, partner, *[blocks[m] for m in range(n) if m not in (late, late + 1)]),
        [shape((2 * rows, half), F32)],
        [pltpu.VMEM((channels, half), BF16)],
        flops=3 * rows * channels * half,
    )
    score, hidden, pre = call(
        functools.partial(forward_kernel, late),
        (embeddings, partner, bias, w_out, begun, blocks[late], blocks[late + 1]),
        [
            shape((groups * n, 2 * rows // LANES, LANES), F32),
            shape((2 * rows, half), BF16),
            shape((2 * rows, half), F32),
        ],
        [pltpu.VMEM((late_window(depth), half), BF16)],
        flops=rows * channels * half,
    )
    received = lax.all_to_all(score, ("grp", "shard"), 0, 0, tiled=True)
    (near,) = call(
        functools.partial(pair_kernel, groups), (received, counts), [shape((rows, 1), F32)], flops=rows * n * rows
    )
    next_to = swap(near, 1)
    message = shape((depth + TAIL, half), jnp.int16)
    first = n // 2
    own_terms, own_sums, slope = call(
        own_kernel,
        (near, flipped, hidden, pre, w_out),
        [shape((channels, half), F32), shape((2, half), F32), shape((rows, half), F32)],
        [pltpu.VMEM((rows, half), BF16)],
        flops=2 * rows * channels * half,
    )
    heads, sent, *distant = call(
        functools.partial(far_kernel, first),
        (next_to, own_terms, own_sums, flipped, hidden, slope, w_out),
        [shape((2, half), F32), shape((rows, half), BF16)] + [message] * (n - first),
        flops=rows * channels * half,
    )
    kept, *close = call(
        near_kernel,
        (heads, sent, own_terms, flipped),
        [shape((depth, half), F32)] + [message] * (first - 1),
        flops=rows * channels * half,
    )
    messages = dict(enumerate(close + distant, 1))
    got = {m: swap(messages[m], m) for m in range(n - 1, 0, -1)}
    sums, tops = call(
        first_sum_kernel,
        (kept, heads, *[got[m] for m in range(1, first)]),
        [shape((2, depth, half), F32), shape((2, 2, half), F32)],
    )
    weight, head = call(
        functools.partial(last_sum_kernel, first),
        (sums, tops, *[got[m] for m in range(first, n)]),
        [shape((depth, hidden_units), F32), shape((2, hidden_units // n), F32)],
    )
    return weight, head.T


def by_collectives(embeddings, w_in, bias, w_out, pair_left, pair_home, pair_remote, outcome):
    local_rows = embeddings.shape[0]
    devices = lax.axis_size("shard")
    pair_count = pair_left.shape[0]
    capacity = 2 * pair_count // devices
    pre = jnp.dot(
        embeddings,
        lax.all_gather(w_in, "shard", axis=0, tiled=True),
        preferred_element_type=jnp.float32,
    )
    pre = pre + bias.astype(jnp.float32)[None, :]
    hidden = activate(pre).astype(jnp.bfloat16)
    part_score = jnp.dot(hidden, w_out, preferred_element_type=jnp.float32)
    score = lax.psum(part_score, "grp")
    home_dev = pair_home[:, 0]
    onehot = (home_dev[:, None] == jnp.arange(devices, dtype=jnp.int32)[None, :]).astype(jnp.int32)
    slot_index = jnp.sum(jnp.cumsum(onehot, axis=0) * onehot, axis=1) - 1
    request = jnp.zeros((devices, capacity), jnp.int32).at[home_dev, slot_index].set(pair_remote)
    wanted = lax.all_to_all(request, "shard", split_axis=0, concat_axis=0, tiled=True)
    wanted_rows = wanted.reshape(-1)
    outgoing = score[wanted_rows].reshape(devices, capacity)
    remote_score = lax.all_to_all(outgoing, "shard", split_axis=0, concat_axis=0, tiled=True)
    margin = score[pair_left] - remote_score[home_dev, slot_index]
    resid = jax.nn.sigmoid(margin) - outcome.astype(jnp.float32)
    backward_slots = (
        jnp.zeros((devices, capacity), jnp.float32).at[home_dev, slot_index].set(-resid)
    )
    returned = lax.all_to_all(backward_slots, "shard", split_axis=0, concat_axis=0, tiled=True)
    dscore = jax.ops.segment_sum(returned.reshape(-1), wanted_rows, num_segments=local_rows)
    dscore = dscore + jax.ops.segment_sum(resid, pair_left, num_segments=local_rows)
    _, pull = jax.vjp(activate, pre)
    dpre32 = pull(dscore[:, None] * w_out.astype(jnp.float32)[None, :])[0]
    dpre = dpre32.astype(jnp.bfloat16)
    grad_bias = jnp.sum(dpre32, axis=0)
    grad_score = jnp.dot(
        dscore, hidden, precision=lax.Precision.HIGHEST, preferred_element_type=jnp.float32
    )
    term_head = jnp.stack([grad_bias, grad_score], axis=1)
    term_weight = lax.dot_general(
        embeddings, dpre, (((0,), (0,)), ((), ())), preferred_element_type=jnp.float32
    )
    return (
        lax.psum_scatter(term_weight, "shard", scatter_dimension=0, tiled=True),
        lax.psum_scatter(term_head, "shard", scatter_dimension=0, tiled=True),
    )


def per_device(embeddings, w_in, bias, w_out, pair_left, pair_home, pair_remote, outcome):
    rows = embeddings.shape[0]
    depth, units = w_in.shape
    n = lax.axis_size("shard")
    small = (
        n & (n - 1) == 0
        and 4 <= n
        and n * rows <= 2048
        and rows % LANES == 0
        and 2 * rows <= 8 * LANES
        and depth % 16 == 0
        and units % (2 * LANES) == 0
        and 2 * depth % (LANES // 2) == 0
        and embeddings.shape[1] == n * depth
        and (n - 2) * depth // LANES * LANES + late_window(depth) <= n * depth
        and pair_left.shape[0] % (16 * LANES) == 0
        and pair_left.shape[0] <= 128 * LANES
        and rows <= 256
    )
    if not small:
        return by_collectives(
            embeddings, w_in, bias, w_out, pair_left, pair_home, pair_remote, outcome
        )
    return by_ppermute(
        embeddings, w_in, bias, w_out, pair_left, pair_home, pair_remote, outcome
    )


def solution(mesh):
    in_specs = (
        P("shard", None),
        P("shard", "grp"),
        P("grp"),
        P("grp"),
        P("shard"),
        P("shard", None),
        P("shard"),
        P("shard"),
    )
    out_specs = (P("shard", "grp"), P(("grp", "shard"), None))
    return jax.shard_map(
        per_device, mesh=mesh, in_specs=in_specs, out_specs=out_specs, check_vma=False
    )
```
